128 devices in a mesh: dp: 4 (over x), seq: 32 (over z, y, core).
Axes of the slice: x: 4, y: 4, z: 4, core: 2. Of those that a mesh axis runs over, the one named last changes fastest.
Arguments:
- inputs: bfloat16 [16384, 6144], P('seq'), may hold values from -6 to 6
- qkv_weight: bfloat16 [6144, 12288], P(None, ('dp', 'seq')), may hold values from -0.078125 to 0.078125
- log_decay: float32 [32, 16384], P('dp', 'seq'), may hold values from -1 to 0, as said below
- out_gain: float32 [32, 128], P('dp'), may hold values from 0.1 to 1.9
Outputs:
- attended: bfloat16 [16384, 4096], P('seq', 'dp')
The draws below stay inside these ranges and needn't reach their ends.
Inputs may be any that keep to these rules, and one draw needn't show every extreme that they name: `log_decay`: log of a decay factor, negative at every position.
All inputs are finite; a program needn't handle non-finite values.
Results may differ from the reference program's by a relative error of at most 0.0055.
Values may be sent and summed in bfloat16 or wider, within the bound.
No kernel may reach another device: no remote copies, remote signals or barrier semaphores. Data moves between devices by JAX's collectives and lax.ppermute only.
A program may use at most 128 MiB of HBM per device.

```python
import jax
import jax.numpy as jnp
from jax import lax

D = 6144
HD = 128
WINDOW_HEADS = 32
TOK_DEV = 512
SEQ_LEN = 16384
QKV = 12288


def draw_inputs(key, part):
    key_list = jax.random.split(key, 2)
    stretch_count = (SEQ_LEN + 127) // 128
    log_scale = jax.random.uniform(key_list[0], (stretch_count, 1), jnp.float32, -2.3, 0.4)
    row_scale = jnp.repeat(jnp.exp(log_scale), 128, axis=0)[:SEQ_LEN]
    standard = jax.random.normal(key_list[1], (SEQ_LEN, D), jnp.float32)
    return jnp.clip(standard * row_scale, -6.0, 6.0).astype(jnp.bfloat16)


def draw_log_decay(key, part):
    every_key_row = jax.random.split(key, 7)
    fast_share = 0.5
    fast_heads = jax.random.uniform(every_key_row[0], (WINDOW_HEADS, 1)) < fast_share
    fast_rate = jnp.exp(jax.random.uniform(every_key_row[1], (WINDOW_HEADS, 1), jnp.float32, jnp.log(1.0 / 50.0), jnp.log(1.0 / 30.0)))
    gradual_rate = jnp.exp(jax.random.uniform(every_key_row[2], (WINDOW_HEADS, 1), jnp.float32, jnp.log(0.05), jnp.log(0.5))) / SEQ_LEN
    default_decay_rate = jnp.where(fast_heads, fast_rate, gradual_rate)
    position_decay_factor = jax.random.uniform(every_key_row[3], (WINDOW_HEADS, SEQ_LEN), jnp.float32, 0.5, 1.5)
    block_decay_factor = jax.random.uniform(every_key_row[4], (WINDOW_HEADS, SEQ_LEN // TOK_DEV), jnp.float32, 0.5, 1.0)
    block_decay_factor = jnp.repeat(block_decay_factor, TOK_DEV, axis=1)
    places = jax.random.randint(every_key_row[5], (WINDOW_HEADS, 2), 0, SEQ_LEN)
    spike_height = jax.random.uniform(every_key_row[6], (WINDOW_HEADS, 2), jnp.float32, 0.22, 0.5)
    positions = jnp.arange(SEQ_LEN)
    agreement_count = (positions[None, :, None] == places[:, None, :]).astype(jnp.float32)
    spike_total_sum = jnp.sum(agreement_count * spike_height[:, None, :], axis=-1)
    return -(default_decay_rate * position_decay_factor * block_decay_factor + spike_total_sum)


def steps_of(own_key, extent, shards, least, top_value):
    def one(dim, shards_of):
        draws = jax.random.uniform(jax.random.fold_in(jax.random.fold_in(own_key, 6), dim), (shards_of,), jnp.float32, least / len(shards), top_value / len(shards))
        return jnp.repeat(jnp.exp(draws), extent[dim] // shards_of).reshape((-1,) + (1,) * (len(extent) - dim - 1))

    loudness = one(*shards[0])
    for cut in shards[1:]:
        loudness = loudness * one(*cut)
    return loudness


def gaussian(key, extent, scale, reach, shards=(), held_as=jnp.bfloat16):
    gain = steps_of(key, extent, shards, -0.22, 0.18) if shards else 1.0
    array = jax.random.normal(key, extent, jnp.float32) * scale * gain
    return jnp.minimum(jnp.maximum(array, -reach), reach).astype(held_as)


def setup_inputs(seed: int = 0) -> dict:
    seeds = jax.random.split(jax.random.key(seed), 5)
    inputs = draw_inputs(jax.random.fold_in(seeds[4], 71), 0)
    qkv_weight = gaussian(seeds[1], (D, QKV), D ** -0.5, 0.078125, ((1, 128),))
    log_decay = draw_log_decay(jax.random.fold_in(seeds[4], 71), 0)
    out_gain = jnp.clip(1.0 + 0.18 * jax.random.normal(seeds[3], (WINDOW_HEADS, HD), jnp.float32), 0.1, 1.9)
    return dict(inputs=inputs, qkv_weight=qkv_weight, log_decay=log_decay, out_gain=out_gain)


def block_terms(queries, keys, values, block_decay):
    cumulated = jnp.cumsum(block_decay, axis=-1)
    tok_count = queries.shape[-2]
    row_index = jnp.arange(tok_count)[:, None]
    col_index = jnp.arange(tok_count)[None, :]
    causal = row_index >= col_index
    spread = cumulated[:, :, None] - cumulated[:, None, :]
    decay_mask = jnp.where(causal, jnp.exp(jnp.where(causal, spread, 0.0)), 0.0)
    scores = jnp.einsum('htd,hsd->hts', queries.astype(jnp.float32), keys.astype(jnp.float32))
    weights = (scores * decay_mask).astype(jnp.bfloat16)
    intra_term = jnp.einsum('hts,hsd->htd', weights.astype(jnp.float32), values.astype(jnp.float32))
    tail_decay = jnp.exp(cumulated[:, -1:] - cumulated)
    keys_decayed = keys.astype(jnp.float32) * tail_decay[:, :, None]
    update = jnp.einsum('hsd,hse->hde', keys_decayed, values.astype(jnp.float32), precision=lax.Precision.HIGHEST)
    block_total = cumulated[:, -1]
    queries_decayed = queries.astype(jnp.float32) * jnp.exp(cumulated)[:, :, None]
    return (intra_term, update, block_total, queries_decayed)

def finish_heads(intra_term, queries_decayed, carried, out_gain):
    outer_term = jnp.einsum('htd,hde->hte', queries_decayed, carried, precision=lax.Precision.HIGHEST)
    combined = intra_term + outer_term
    root_mean = lax.rsqrt(lax.optimization_barrier(jnp.mean(combined * combined, axis=-1, keepdims=True)) + 1e-05)
    return combined * root_mean * out_gain[:, None, :]

def reference(inputs, qkv_weight, log_decay, out_gain):
    block_count = SEQ_LEN // TOK_DEV
    blocks_in = inputs.reshape(block_count, TOK_DEV, D)
    blocks_decay = jnp.transpose(log_decay.reshape(WINDOW_HEADS, block_count, TOK_DEV), (1, 0, 2))

    def advance(carried, block_item):
        block_in, block_decay = block_item
        projected = jnp.dot(block_in, qkv_weight, preferred_element_type=jnp.float32)
        activated = jax.nn.silu(projected).astype(jnp.bfloat16).reshape(TOK_DEV, WINDOW_HEADS, 3, HD)
        activated = jnp.transpose(activated, (2, 1, 0, 3))
        intra_term, update, block_total, queries_decayed = block_terms(activated[0], activated[1], activated[2], block_decay)
        normed = finish_heads(intra_term, queries_decayed, carried, out_gain)
        renewed = jnp.exp(block_total)[:, None, None] * carried + update
        result = jnp.transpose(normed, (1, 0, 2)).reshape(TOK_DEV, WINDOW_HEADS * HD).astype(jnp.bfloat16)
        return (renewed, result)
    start_state = jnp.zeros((WINDOW_HEADS, HD, HD), jnp.float32)
    _, results = lax.scan(advance, start_state, (blocks_in, blocks_decay))
    return results.reshape(SEQ_LEN, WINDOW_HEADS * HD)
```

```python
import functools

import jax
import jax.numpy as jnp
from jax import lax
from jax.experimental import pallas as pl
from jax.experimental.pallas import tpu as pltpu
from jax.sharding import Mesh
from jax.sharding import PartitionSpec as P


F32 = jnp.float32
BF16 = jnp.bfloat16
TOK = 512
DIM = 6144
UNIT = 96
KB = 768
NK = DIM // KB
SPLIT = 3
GROUP = ("zl", "y", "c")


def ring_pairs(step):
    return [
        (i * 2 + c, ((i + (step if c == 0 else -step)) % 4) * 2 + c) for i in range(4) for c in range(2)
    ]


def y_move(v, step):
    return lax.ppermute(v, ("y", "c"), ring_pairs(step))


def x_move(v, step):
    return lax.ppermute(v, ("x", "c"), ring_pairs(step))


def z_in(v):
    return lax.ppermute(v, "zl", [(0, 1), (1, 0)])


def z_out(v):
    return lax.ppermute(v, ("zh", "zl"), [(i, 3 - i) for i in range(4)])


def core_swap(v):
    return lax.ppermute(v, "c", [(0, 1), (1, 0)])


def project(scalars, xs, ws, held, block):
    units = len(ws)
    pieces = len(xs) > 1

    def kernel(s_ref, *refs):
        x_refs, refs = refs[: len(xs)], refs[len(xs) :]
        w_refs, refs = refs[:units], refs[units:]
        if held is not None:
            refs = refs[1:]
        u_ref, acc, stage, sem = refs[:4]
        k = pl.program_id(0)
        if pieces:
            buf = refs[4]
            for p in range(4):
                row = pl.multiple_of(s_ref[units + p] * 128, 128)

                @pl.when(k < SPLIT)
                def _():
                    buf[pl.ds(row, 128), :] = x_refs[p][...]

                @pl.when(k >= SPLIT)
                def _():
                    buf[pl.ds(row, 128), :] = x_refs[4 + p][...]

            x = buf[...]
        else:
            x = x_refs[0][...]
        w = jnp.concatenate([r[...] for r in w_refs], axis=0)
        part = lax.dot_general(w, x, (((1,), (1,)), ((), ())), preferred_element_type=F32)

        @pl.when(k == 0)
        def _():
            acc[...] = part

        @pl.when(k > 0)
        def _():
            acc[...] += part

        @pl.when(k == NK - 1)
        def _():
            copies = []
            for i in range(units):
                rows = slice(i * UNIT, (i + 1) * UNIT)
                v = acc[rows, :]
                stage[rows, :] = (v * jax.nn.sigmoid(v)).astype(BF16)
                at = pl.multiple_of(s_ref[i] * UNIT, UNIT)
                copy = pltpu.make_async_copy(
                    stage.at[rows, :],
                    u_ref.at[pl.ds(at, UNIT), block * TOK : (block + 1) * TOK],
                    sem.at[i],
                )
                copy.start()
                copies.append(copy)
            for copy in copies:
                copy.wait()

    if pieces:
        x_specs = [pl.BlockSpec((128, KB), lambda k, s: (0, jnp.minimum(k, SPLIT - 1)))] * 4
        x_specs += [pl.BlockSpec((128, KB), lambda k, s: (0, jnp.maximum(k - SPLIT, 0)))] * 4
    else:
        x_specs = [pl.BlockSpec((TOK, KB), lambda k, s: (0, k))]
    in_specs = x_specs + [pl.BlockSpec((UNIT, KB), lambda k, s: (0, k))] * units
    scratch = [
        pltpu.VMEM((units * UNIT, TOK), F32),
        pltpu.VMEM((units * UNIT, TOK), BF16),
        pltpu.SemaphoreType.DMA((units,)),
    ]
    if pieces:
        scratch.append(pltpu.VMEM((TOK, KB), BF16))
    args = [scalars, *xs, *ws]
    aliases = {}
    if held is not None:
        in_specs.append(pl.BlockSpec(memory_space=pl.ANY))
        aliases = {len(args): 0}
        args.append(held)
    return pl.pallas_call(
        kernel,
        grid_spec=pltpu.PrefetchScalarGridSpec(
            num_scalar_prefetch=1,
            grid=(NK,),
            in_specs=in_specs,
            out_specs=pl.BlockSpec(memory_space=pl.ANY),
            scratch_shapes=scratch,
        ),
        out_shape=jax.ShapeDtypeStruct((16 * UNIT, 2 * TOK), BF16),
        input_output_aliases=aliases,
        cost_estimate=pl.CostEstimate(
            flops=2 * units * UNIT * TOK * DIM,
            bytes_accessed=2 * DIM * (units * UNIT + TOK),
            transcendentals=units * UNIT * TOK,
        ),
        name="project",
    )(*args)


def column(kind):
    return pl.BlockSpec((128, TOK), lambda i: ((i % 4) * 3 + kind, i // 4))


ROW = pl.BlockSpec((1, 1, TOK), lambda i: (i, 0, 0))
STATE = pl.BlockSpec((4, 1, 32, 128), lambda i: (i % 4, i // 4, 0, 0))


def states(held, cumulated):
    def kernel(k_ref, v_ref, c_ref, o_ref):
        cum = c_ref[0]
        tail = jnp.exp(cum[:, TOK - 1 :] - cum)
        k = k_ref[...].astype(F32) * tail
        high = k.astype(BF16)
        low = (k - high.astype(F32)).astype(BF16)
        v = v_ref[...]
        dims = (((1,), (1,)), ((), ()))
        update = lax.dot_general(high, v, dims, preferred_element_type=F32)
        update += lax.dot_general(low, v, dims, preferred_element_type=F32)
        o_ref[...] = update.astype(BF16).reshape(4, 1, 32, 128)

    return pl.pallas_call(
        kernel,
        grid=(8,),
        in_specs=[column(1), column(2), ROW],
        out_specs=STATE,
        out_shape=jax.ShapeDtypeStruct((16, 2, 32, 128), BF16),
        name="states",
    )(held, held, cumulated)


def intra(held, cumulated):
    def kernel(q_ref, k_ref, v_ref, c_ref, o_ref):
        cum = c_ref[0]
        cum_col = jnp.transpose(jnp.broadcast_to(cum, (128, TOK)))
        for j in range(4):
            lanes = slice(j * 128, (j + 1) * 128)
            count = (j + 1) * 128
            scores = lax.dot_general(
                k_ref[:, :count], q_ref[:, lanes], (((0,), (0,)), ((), ())), preferred_element_type=F32
            )
            spread = cum[:, lanes] - cum_col[:count]
            s = lax.broadcasted_iota(jnp.int32, (count, 128), 0)
            t = lax.broadcasted_iota(jnp.int32, (count, 128), 1) + j * 128
            decay = jnp.exp(jnp.where(s <= t, spread, -1e30))
            weights = (scores * decay).astype(BF16)
            o_ref[0, :, lanes] = jnp.dot(v_ref[:, :count], weights, preferred_element_type=F32)

    return pl.pallas_call(
        kernel,
        grid=(8,),
        in_specs=[column(0), column(1), column(2), ROW],
        out_specs=pl.BlockSpec((1, 128, TOK), lambda i: (i, 0, 0)),
        out_shape=jax.ShapeDtypeStruct((8, 128, TOK), F32),
        name="intra",
    )(held, held, held, cumulated)


def carries(order, decays, pieces):
    def kernel(n_ref, d_ref, s_ref, o_ref):
        state = jnp.zeros((32, 128), F32)
        for b in range(32):
            z, yc = b // 8, b % 8
            source = n_ref[2 * z] * 8 + yc
            block = n_ref[2 * z + 1]
            o_ref[source, block] = state.astype(BF16)
            state = d_ref[source, block] * state + s_ref[source, block].astype(F32)

    return pl.pallas_call(
        kernel,
        in_specs=[
            pl.BlockSpec(memory_space=pltpu.SMEM),
            pl.BlockSpec(memory_space=pltpu.SMEM),
            pl.BlockSpec(memory_space=pltpu.VMEM),
        ],
        out_specs=pl.BlockSpec(memory_space=pltpu.VMEM),
        out_shape=jax.ShapeDtypeStruct((16, 2, 32, 128), BF16),
        name="carries",
    )(order, decays, pieces)


def finish(held, cumulated, inside, carried, gains, block):
    def kernel(q_ref, c_ref, i_ref, s_ref, g_ref, o_ref):
        carry = s_ref[...].reshape(128, 128)
        outer = lax.dot_general(carry, q_ref[...], (((0,), (0,)), ((), ())), preferred_element_type=F32)
        combined = i_ref[0] + outer * jnp.exp(c_ref[0])
        root = lax.rsqrt(jnp.mean(combined * combined, axis=0, keepdims=True) + 1e-05)
        o_ref[...] = jnp.transpose(combined * root * g_ref[0]).astype(BF16)

    return pl.pallas_call(
        kernel,
        grid=(4,),
        in_specs=[
            pl.BlockSpec((128, TOK), lambda i: (i * 3, block)),
            pl.BlockSpec((1, 1, TOK), lambda i: (i + 4 * block, 0, 0)),
            pl.BlockSpec((1, 128, TOK), lambda i: (i + 4 * block, 0, 0)),
            pl.BlockSpec((4, 1, 32, 128), lambda i: (i, block, 0, 0)),
            pl.BlockSpec((1, 128, 1), lambda i: (i, 0, 0)),
        ],
        out_specs=pl.BlockSpec((TOK, 128), lambda i: (0, i)),
        out_shape=jax.ShapeDtypeStruct((TOK, 512), BF16),
        name="finish",
    )(held, cumulated, inside, carried, gains)


def shards(inputs, qkv_weight, log_decay, out_gain):
    x = lax.axis_index("x")
    zh = lax.axis_index("zh")
    zl = lax.axis_index("zl")
    y = lax.axis_index("y")
    c = lax.axis_index("c")
    side = 1 - 2 * c

    own = qkv_weight.T
    quarter = lax.dynamic_slice(inputs, (128 * x, 0), (128, DIM))
    cut = SPLIT * KB
    a0 = z_out(quarter[:, :cut])
    w_a = y_move(own, 1)
    w_b = y_move(own, -1)
    w_z = z_in(own)
    a1 = z_out(quarter[:, cut:])
    s_own = core_swap(own)
    log_decay_across = z_out(log_decay)
    xa0, xb0 = x_move(a0, 1), x_move(a0, -1)
    w_c = y_move(w_a, 1)
    w_zb = y_move(w_z, -1)
    w_za = z_in(w_a)
    s_a, s_b, s_z = core_swap(w_a), core_swap(w_b), core_swap(w_z)
    xc0 = x_move(xa0, 1)
    xa1, xb1 = x_move(a1, 1), x_move(a1, -1)
    w_zbb = y_move(w_zb, -1)
    s_c, s_zb, s_za = core_swap(w_c), core_swap(w_zb), core_swap(w_za)
    xc1 = x_move(xa1, 1)
    s_zbb = core_swap(w_zbb)

    def unit(row, shift, core):
        return (row * 4 + (y + shift) % 4) * 2 + core

    zi, cs = 1 - zl, 1 - c
    first = [
        (own, unit(zl, 0, c)),
        (s_own, unit(zl, 0, cs)),
        (w_a, unit(zl, -side, c)),
        (s_a, unit(zl, side, cs)),
        (w_b, unit(zl, side, c)),
        (s_b, unit(zl, -side, cs)),
        (w_z, unit(zi, 0, c)),
        (s_z, unit(zi, 0, cs)),
    ]
    second = [
        (w_c, unit(zl, 2, c)),
        (s_c, unit(zl, 2, cs)),
        (w_za, unit(zi, -side, c)),
        (s_za, unit(zi, side, cs)),
        (w_zb, unit(zi, side, c)),
        (s_zb, unit(zi, -side, cs)),
    ]
    third = [(w_zbb, unit(zi, 2, c)), (s_zbb, unit(zi, 2, cs))]
    places = [x, (x - side) % 4, (x + side) % 4, (x + 2) % 4]
    across = [a0, xa0, xb0, xc0, a1, xa1, xb1, xc1]

    def run(xs, units, held, block, extra=()):
        scalars = jnp.stack([n for _, n in units] + list(extra)).astype(jnp.int32)
        return project(scalars, xs, [w for w, _ in units], held, block)

    held = run([inputs], first, None, 0)
    held = run([inputs], second, held, 0)
    held = run(across, first + second, held, 1, places)
    held = run([inputs], third, held, 0)
    held = run(across, third, held, 1, places)

    rates = jnp.stack([log_decay, log_decay_across])
    rates = lax.dynamic_slice(rates, (0, 4 * zh, 0), (2, 4, TOK))
    cumulated = jnp.cumsum(rates, axis=-1)
    totals = cumulated[:, :, -1]
    parts = jnp.repeat(totals.T, 4, axis=0)
    decays = jnp.exp(lax.all_to_all(parts, GROUP, 0, 0, tiled=True))
    cumulated = cumulated.reshape(8, 1, TOK)
    order = jnp.where(zh == 0, jnp.array([0, 0, 1, 0, 1, 1, 0, 1]), jnp.array([1, 1, 0, 1, 0, 0, 1, 0]))
    gains = lax.dynamic_slice(out_gain, (4 * zh, 0), (4, 128)).reshape(4, 128, 1)

    update = lax.all_to_all(states(held, cumulated), GROUP, 0, 0, tiled=True)
    inside = intra(held, cumulated)
    carried = lax.all_to_all(carries(order.astype(jnp.int32), decays, update), GROUP, 0, 0, tiled=True)
    over = z_out(finish(held, cumulated, inside, carried, gains, 1))
    here = finish(held, cumulated, inside, carried, gains, 0)
    return jnp.where(zh == 0, jnp.concatenate([here, over], 1), jnp.concatenate([over, here], 1))


def solution(mesh):
    fine = Mesh(mesh.devices.reshape(4, 2, 2, 4, 2), ("x", "zh", "zl", "y", "c"))
    seq = ("zh", "zl", "y", "c")
    in_specs = (P(seq, None), P(None, ("x",) + seq), P("x", seq), P("x", None))
    return jax.shard_map(shards, mesh=fine, in_specs=in_specs, out_specs=P(seq, "x"), check_vma=False)
```

```python
import jax
import jax.numpy as jnp
from jax import lax
from jax.experimental import pallas as pl
from jax.experimental.pallas import tpu as pltpu
from jax.sharding import Mesh
from jax.sharding import PartitionSpec as P


F32 = jnp.float32
BF16 = jnp.bfloat16
TOK = 512
DIM = 6144
UNIT = 96
KB = 2048
NK = DIM // KB
SPLIT = 1
GROUP = ("zl", "y", "c")


def ring_pairs(step):
    return [
        (i * 2 + c, ((i + (step if c == 0 else -step)) % 4) * 2 + c) for i in range(4) for c in range(2)
    ]


def y_move(v, step):
    return lax.ppermute(v, ("y", "c"), ring_pairs(step))


def x_move(v, step):
    return lax.ppermute(v, ("x", "c"), ring_pairs(step))


def z_in(v):
    return lax.ppermute(v, "zl", [(0, 1), (1, 0)])


def z_out(v):
    return lax.ppermute(v, ("zh", "zl"), [(i, 3 - i) for i in range(4)])


def core_swap(v):
    return lax.ppermute(v, "c", [(0, 1), (1, 0)])


def project(scalars, tokens, units, jobs, held):
    flat = [a for arrays, _ in tokens for a in arrays]
    sizes = [arrays[0].shape[0] for arrays, _ in tokens]
    copies_of = sum(len(g) * len(u) for g, u in jobs)

    def kernel(s_ref, *refs):
        x_refs, refs = list(refs[: len(flat)]), refs[len(flat) :]
        w_refs, refs = refs[: len(units)], refs[len(units) :]
        if held is not None:
            refs = refs[1:]
        u_ref, sem, refs = refs[0], refs[1], refs[2:]
        accs, stages, bufs = refs[: len(jobs)], refs[len(jobs) : 2 * len(jobs)], list(refs[2 * len(jobs) :])
        k = pl.program_id(0)
        values = []
        for arrays, _ in tokens:
            if len(arrays) == 1:
                values.append(x_refs.pop(0)[...])
                continue
            early, late, buf = x_refs.pop(0), x_refs.pop(0), bufs.pop(0)

            @pl.when(k < SPLIT)
            def _():
                buf[...] = early[...]

            @pl.when(k >= SPLIT)
            def _():
                buf[...] = late[...]

            values.append(buf[...])
        for (groups, members), acc in zip(jobs, accs):
            x = jnp.concatenate([values[g] for g in groups], axis=0)
            w = jnp.concatenate([w_refs[m][...] for m in members], axis=0)
            part = lax.dot_general(w, x, (((1,), (1,)), ((), ())), preferred_element_type=F32)

            @pl.when(k == 0)
            def _():
                acc[...] = part

            @pl.when(k > 0)
            def _():
                acc[...] += part

        @pl.when(k == NK - 1)
        def _():
            copies = []
            for (groups, members), acc, stage in zip(jobs, accs, stages):
                for i, m in enumerate(members):
                    rows = slice(i * UNIT, (i + 1) * UNIT)
                    v = acc[rows, :]
                    stage[rows, :] = (v * jax.nn.sigmoid(v)).astype(BF16)
                    at = pl.multiple_of(s_ref[units[m][1]] * UNIT, UNIT)
                    start = 0
                    for g in groups:
                        lane = tokens[g][1]
                        size = sizes[g]
                        if size == 128:
                            lane = pl.multiple_of(s_ref[lane] * 128, 128)
                        copy = pltpu.make_async_copy(
                            stage.at[rows, start : start + size],
                            u_ref.at[pl.ds(at, UNIT), pl.ds(lane, size)],
                            sem.at[len(copies)],
                        )
                        copy.start()
                        copies.append(copy)
                        start += size
            for copy in copies:
                copy.wait()

    in_specs = []
    for arrays, _ in tokens:
        rows = arrays[0].shape[0]
        if len(arrays) == 1:
            in_specs.append(pl.BlockSpec((rows, KB), lambda k, s: (0, k)))
        else:
            in_specs.append(pl.BlockSpec((rows, KB), lambda k, s: (0, jnp.minimum(k, SPLIT - 1))))
            in_specs.append(pl.BlockSpec((rows, KB), lambda k, s: (0, jnp.maximum(k - SPLIT, 0))))
    in_specs += [pl.BlockSpec((UNIT, KB), lambda k, s: (0, k))] * len(units)
    shapes = [(len(u) * UNIT, sum(sizes[g] for g in gs)) for gs, u in jobs]
    scratch = [pltpu.SemaphoreType.DMA((copies_of,))]
    scratch += [pltpu.VMEM(shape, F32) for shape in shapes]
    scratch += [pltpu.VMEM(shape, BF16) for shape in shapes]
    scratch += [pltpu.VMEM((128, KB), BF16) for arrays, _ in tokens if len(arrays) == 2]
    args = [scalars, *flat, *[w for w, _ in units]]
    aliases = {}
    if held is not None:
        in_specs.append(pl.BlockSpec(memory_space=pl.ANY))
        aliases = {len(args): 0}
        args.append(held)
    products = sum(a * b for a, b in shapes)
    return pl.pallas_call(
        kernel,
        grid_spec=pltpu.PrefetchScalarGridSpec(
            num_scalar_prefetch=1,
            grid=(NK,),
            in_specs=in_specs,
            out_specs=pl.BlockSpec(memory_space=pl.ANY),
            scratch_shapes=scratch,
        ),
        out_shape=jax.ShapeDtypeStruct((16 * UNIT, 2 * TOK), BF16),
        input_output_aliases=aliases,
        cost_estimate=pl.CostEstimate(
            flops=2 * products * DIM,
            bytes_accessed=2 * DIM * (len(units) * UNIT + sum(sizes)),
            transcendentals=products,
        ),
        name="project",
    )(*args)


def heads_of(kind):
    return [pl.BlockSpec((128, 2 * TOK), lambda i, h=h: (h * 3 + kind, 0)) for h in range(4)]


def whole(shape):
    return pl.BlockSpec(shape, lambda i: (0,) * len(shape))


def states(held, cumulated):
    def kernel(*refs):
        k_refs, v_refs, c_ref, o_ref = refs[:4], refs[4:8], refs[8], refs[9]
        dims = (((1,), (1,)), ((), ()))
        for block in range(2):
            lanes = slice(block * TOK, (block + 1) * TOK)
            for h in range(4):
                cum = c_ref[block * 4 + h]
                tail = jnp.exp(cum[:, TOK - 1 :] - cum)
                k = k_refs[h][:, lanes].astype(F32) * tail
                high = k.astype(BF16)
                low = (k - high.astype(F32)).astype(BF16)
                v = v_refs[h][:, lanes]
                update = lax.dot_general(high, v, dims, preferred_element_type=F32)
                update += lax.dot_general(low, v, dims, preferred_element_type=F32)
                o_ref[h * 4 : h * 4 + 4, block] = update.astype(BF16).reshape(4, 32, 128)

    return pl.pallas_call(
        kernel,
        grid=(1,),
        in_specs=heads_of(1) + heads_of(2) + [whole((8, 1, TOK))],
        out_specs=whole((16, 2, 32, 128)),
        out_shape=jax.ShapeDtypeStruct((16, 2, 32, 128), BF16),
        name="states",
    )(*[held] * 8, cumulated)


def intra(held, cumulated, block):
    def kernel(*refs):
        q_refs, k_refs, v_refs, c_ref, o_ref = refs[:4], refs[4:8], refs[8:12], refs[12], refs[13]
        for h in range(4):
            cum = c_ref[h]
            cum_col = jnp.transpose(jnp.broadcast_to(cum, (128, TOK)))
            for j in range(4):
                lanes = slice(j * 128, (j + 1) * 128)
                count = (j + 1) * 128
                scores = lax.dot_general(
                    k_refs[h][:, :count],
                    q_refs[h][:, lanes],
                    (((0,), (0,)), ((), ())),
                    preferred_element_type=F32,
                )
                spread = cum[:, lanes] - cum_col[:count]
                s = lax.broadcasted_iota(jnp.int32, (count, 128), 0)
                t = lax.broadcasted_iota(jnp.int32, (count, 128), 1) + j * 128
                decay = jnp.exp(jnp.where(s <= t, spread, -1e30))
                weights = (scores * decay).astype(BF16)
                o_ref[h, :, lanes] = jnp.dot(v_refs[h][:, :count], weights, preferred_element_type=F32)

    return pl.pallas_call(
        kernel,
        grid=(1,),
        in_specs=[
            pl.BlockSpec((128, TOK), lambda i, h=h, kind=kind: (h * 3 + kind, block))
            for kind in range(3)
            for h in range(4)
        ]
        + [pl.BlockSpec((4, 1, TOK), lambda i: (block, 0, 0))],
        out_specs=whole((4, 128, TOK)),
        out_shape=jax.ShapeDtypeStruct((4, 128, TOK), F32),
        name="intra",
    )(*[held] * 12, cumulated)


def carries(order, decays, pieces):
    def kernel(n_ref, d_ref, s_ref, o_ref):
        state = jnp.zeros((32, 128), F32)
        for b in range(32):
            z, yc = b // 8, b % 8
            source = n_ref[2 * z] * 8 + yc
            block = n_ref[2 * z + 1]
            o_ref[source, block] = state.astype(BF16)
            state = d_ref[source, block] * state + s_ref[source, block].astype(F32)

    return pl.pallas_call(
        kernel,
        in_specs=[
            pl.BlockSpec(memory_space=pltpu.SMEM),
            pl.BlockSpec(memory_space=pltpu.SMEM),
            pl.BlockSpec(memory_space=pltpu.VMEM),
        ],
        out_specs=pl.BlockSpec(memory_space=pltpu.VMEM),
        out_shape=jax.ShapeDtypeStruct((16, 2, 32, 128), BF16),
        name="carries",
    )(order, decays, pieces)


def finish(held, cumulated, inside, carried, gains, block):
    def kernel(*refs):
        q_refs, c_ref, i_ref, s_ref, g_ref, o_ref = refs[:4], *refs[4:]
        for h in range(4):
            carry = s_ref[4 * h : 4 * h + 4, 0].reshape(128, 128)
            outer = lax.dot_general(
                carry, q_refs[h][...], (((0,), (0,)), ((), ())), preferred_element_type=F32
            )
            combined = i_ref[h] + outer * jnp.exp(c_ref[h])
            root = lax.rsqrt(jnp.mean(combined * combined, axis=0, keepdims=True) + 1e-05)
            o_ref[:, h * 128 : (h + 1) * 128] = jnp.transpose(combined * root * g_ref[h]).astype(BF16)

    return pl.pallas_call(
        kernel,
        grid=(1,),
        in_specs=[pl.BlockSpec((128, TOK), lambda i, h=h: (h * 3, block)) for h in range(4)]
        + [
            pl.BlockSpec((4, 1, TOK), lambda i: (block, 0, 0)),
            whole((4, 128, TOK)),
            pl.BlockSpec((16, 1, 32, 128), lambda i: (0, block, 0, 0)),
            whole((4, 128, 1)),
        ],
        out_specs=whole((TOK, 512)),
        out_shape=jax.ShapeDtypeStruct((TOK, 512), BF16),
        name="finish",
    )(*[held] * 4, cumulated, inside, carried, gains)


def shards(inputs, qkv_weight, log_decay, out_gain):
    x = lax.axis_index("x")
    zh = lax.axis_index("zh")
    zl = lax.axis_index("zl")
    y = lax.axis_index("y")
    c = lax.axis_index("c")
    side = 1 - 2 * c

    log_decay_across = z_out(log_decay)
    rates = jnp.stack([log_decay, log_decay_across])
    rates = lax.dynamic_slice(rates, (0, 4 * zh, 0), (2, 4, TOK))
    cumulated = jnp.cumsum(rates, axis=-1)
    totals = cumulated[:, :, -1]
    parts = jnp.repeat(totals.T, 4, axis=0)
    decays = jnp.exp(lax.all_to_all(parts, GROUP, 0, 0, tiled=True))
    cumulated = cumulated.reshape(8, 1, TOK)
    order = jnp.where(zh == 0, jnp.array([0, 0, 1, 0, 1, 1, 0, 1]), jnp.array([1, 1, 0, 1, 0, 0, 1, 0]))
    order = order.astype(jnp.int32)
    gains = lax.dynamic_slice(out_gain, (4 * zh, 0), (4, 128)).reshape(4, 128, 1)

    def unit(row, shift, core):
        return (row * 4 + (y + shift) % 4) * 2 + core

    zi, cs = 1 - zl, 1 - c
    rows = [
        unit(zl, 0, c),
        unit(zl, 0, cs),
        unit(zl, -side, c),
        unit(zl, side, cs),
        unit(zl, side, c),
        unit(zl, -side, cs),
        unit(zi, 0, c),
        unit(zi, 0, cs),
        unit(zl, 2, c),
        unit(zl, 2, cs),
        unit(zi, -side, c),
        unit(zi, side, cs),
        unit(zi, side, c),
        unit(zi, -side, cs),
        unit(zi, 2, c),
        unit(zi, 2, cs),
    ]
    lanes = [4 + q % 4 for q in (x, x - side, x + side, x + 2)]
    scalars = jnp.stack(rows + lanes).astype(jnp.int32)

    own = qkv_weight.T
    quarter = lax.dynamic_slice(inputs, (128 * x, 0), (128, DIM))
    cut = SPLIT * KB
    w_a = y_move(own, 1)
    w_b = y_move(own, -1)
    w_z = z_in(own)
    a0 = z_out(quarter[:, :cut])
    a1 = z_out(quarter[:, cut:])
    s_own = core_swap(own)
    small = (cumulated, decays, order, gains, scalars)
    a0, (cumulated, decays, order, gains, scalars) = lax.optimization_barrier((a0, small))
    xa0 = x_move(a0, 1)
    xb0 = x_move(a0, -1)
    w_c = y_move(w_a, 1)
    w_zb = y_move(w_z, -1)
    w_za = z_in(w_a)
    s_a = core_swap(w_a)
    s_b = core_swap(w_b)
    s_z = core_swap(w_z)
    xc0 = x_move(xa0, 1)
    xa1 = x_move(a1, 1)
    xb1 = x_move(a1, -1)
    w_zbb = y_move(w_zb, -1)
    s_c = core_swap(w_c)
    s_zb = core_swap(w_zb)
    s_za = core_swap(w_za)
    xc1 = x_move(xa1, 1)
    s_zbb = core_swap(w_zbb)

    weights = [own, s_own, w_a, s_a, w_b, s_b, w_z, s_z, w_c, s_c, w_za, s_za, w_zb, s_zb, w_zbb, s_zbb]
    units = [(w, i) for i, w in enumerate(weights)]
    here = ([inputs], 0)
    across = [([a0, a1], 16), ([xa0, xa1], 17), ([xb0, xb1], 18), ([xc0, xc1], 19)]
    held = project(scalars, [here], units[:8], [((0,), range(8))], None)
    jobs = [((0,), range(8, 14)), ((1, 2, 3), range(14))]
    held = project(scalars, [here] + across[:3], units[:14], jobs, held)
    jobs = [((0, 1, 2, 3), (14, 15)), ((4,), range(16))]
    held = project(scalars, [here] + across, units, jobs, held)

    own_states = states(held, cumulated)
    update = lax.all_to_all(own_states, GROUP, 0, 0, tiled=True)
    held, _ = lax.optimization_barrier((held, own_states))
    inside_across = intra(held, cumulated, 1)
    update, inside_across = lax.optimization_barrier((update, inside_across))
    running = carries(order, decays, update)
    carried = lax.all_to_all(running, GROUP, 0, 0, tiled=True)
    held, _ = lax.optimization_barrier((held, running))
    inside = intra(held, cumulated, 0)
    carried, inside = lax.optimization_barrier((carried, inside))
    over = z_out(finish(held, cumulated, inside_across, carried, gains, 1))
    here = finish(held, cumulated, inside, carried, gains, 0)
    return jnp.where(zh == 0, jnp.concatenate([here, over], 1), jnp.concatenate([over, here], 1))


def solution(mesh):
    fine = Mesh(mesh.devices.reshape(4, 2, 2, 4, 2), ("x", "zh", "zl", "y", "c"))
    seq = ("zh", "zl", "y", "c")
    in_specs = (P(seq, None), P(None, ("x",) + seq), P("x", seq), P("x", None))
    return jax.shard_map(shards, mesh=fine, in_specs=in_specs, out_specs=P(seq, "x"), check_vma=False)
```

```python
import jax
import jax.numpy as jnp
from jax import lax
from jax.experimental import pallas as pl
from jax.experimental.pallas import tpu as pltpu
from jax.sharding import Mesh
from jax.sharding import PartitionSpec as P


F32 = jnp.float32
BF16 = jnp.bfloat16
TOK = 512
DIM = 6144
UNIT = 96
KB = 1536
NK = DIM // KB
SPLIT = 2
GROUP = ("zl", "y", "c")
SEQ = ("zh", "zl", "y", "c")


def ring_pairs(step):
    return [
        (i * 2 + c, ((i + (step if c == 0 else -step)) % 4) * 2 + c) for i in range(4) for c in range(2)
    ]


def y_move(v, step):
    return lax.ppermute(v, ("y", "c"), ring_pairs(step))


def x_move(v, step):
    return lax.ppermute(v, ("x", "c"), ring_pairs(step))


def z_in(v):
    return lax.ppermute(v, "zl", [(0, 1), (1, 0)])


def z_out(v):
    return lax.ppermute(v, ("zh", "zl"), [(i, 3 - i) for i in range(4)])


def exchange(v, axes):
    return lax.all_to_all(v, axes, 0, 0, tiled=True)


def core_swap(v):
    return lax.ppermute(v, "c", [(0, 1), (1, 0)])


def project(scalars, blocks, units, jobs, held):
    flat = [a for arrays in blocks for a in arrays]
    count = sum(len(u) for _, u in jobs)
    both = len(blocks) == 2

    def kernel(s_ref, *refs):
        x_refs, refs = refs[: len(flat)], refs[len(flat) :]
        w_refs, refs = refs[: len(units)], refs[len(units) :]
        if held is not None:
            refs = refs[1:]
        u_ref, sem, refs = refs[0], refs[1], refs[2:]
        accs, stages, refs = refs[: len(jobs)], refs[len(jobs) : 2 * len(jobs)], refs[2 * len(jobs) :]
        k = pl.program_id(0)
        values = [x_refs[0]]
        if both:
            buf = refs[0]
            for p in range(4):
                row = pl.multiple_of(s_ref[16 + p] * 128, 128)

                @pl.when(k < SPLIT)
                def _():
                    buf[pl.ds(row, 128), :] = x_refs[1 + p][...]

                @pl.when(k >= SPLIT)
                def _():
                    buf[pl.ds(row, 128), :] = x_refs[5 + p][...]

            values.append(buf)
        for (block, members), acc in zip(jobs, accs):
            w = jnp.concatenate([w_refs[m][...] for m in members], axis=0)
            part = lax.dot_general(
                w, values[block][...], (((1,), (1,)), ((), ())), preferred_element_type=F32
            )

            @pl.when(k == 0)
            def _():
                acc[...] = part

            @pl.when(k > 0)
            def _():
                acc[...] += part

        @pl.when(k == NK - 1)
        def _():
            copies = []
            for (block, members), acc, stage in zip(jobs, accs, stages):
                for i, m in enumerate(members):
                    rows = slice(i * UNIT, (i + 1) * UNIT)
                    v = acc[rows, :]
                    stage[rows, :] = (v * jax.nn.sigmoid(v)).astype(BF16)
                    at = pl.multiple_of(s_ref[units[m][1]] * UNIT, UNIT)
                    copy = pltpu.make_async_copy(
                        stage.at[rows, :],
                        u_ref.at[pl.ds(at, UNIT), block * TOK : (block + 1) * TOK],
                        sem.at[len(copies)],
                    )
                    copy.start()
                    copies.append(copy)
            for copy in copies:
                copy.wait()

    in_specs = [pl.BlockSpec((TOK, KB), lambda k, s: (0, k))]
    if both:
        in_specs += [pl.BlockSpec((128, KB), lambda k, s: (0, jnp.minimum(k, SPLIT - 1)))] * 4
        in_specs += [pl.BlockSpec((128, KB), lambda k, s: (0, jnp.maximum(k - SPLIT, 0)))] * 4
    in_specs += [pl.BlockSpec((UNIT, KB), lambda k, s: (0, k))] * len(units)
    scratch = [pltpu.SemaphoreType.DMA((count,))]
    scratch += [pltpu.VMEM((len(u) * UNIT, TOK), F32) for _, u in jobs]
    scratch += [pltpu.VMEM((len(u) * UNIT, TOK), BF16) for _, u in jobs]
    if both:
        scratch.append(pltpu.VMEM((TOK, KB), BF16))
    args = [scalars, *flat, *[w for w, _ in units]]
    aliases = {}
    if held is not None:
        in_specs.append(pl.BlockSpec(memory_space=pl.ANY))
        aliases = {len(args): 0}
        args.append(held)
    return pl.pallas_call(
        kernel,
        grid_spec=pltpu.PrefetchScalarGridSpec(
            num_scalar_prefetch=1,
            grid=(NK,),
            in_specs=in_specs,
            out_specs=pl.BlockSpec(memory_space=pl.ANY),
            scratch_shapes=scratch,
        ),
        out_shape=jax.ShapeDtypeStruct((16 * UNIT, 2 * TOK), BF16),
        input_output_aliases=aliases,
        cost_estimate=pl.CostEstimate(
            flops=2 * count * UNIT * TOK * DIM,
            bytes_accessed=2 * DIM * (len(units) * UNIT + TOK * len(blocks)),
            transcendentals=count * UNIT * TOK,
        ),
        name="project",
    )(*args)


SMEM = pl.BlockSpec(memory_space=pltpu.SMEM)


def running_sum(v):
    lane = lax.broadcasted_iota(jnp.int32, v.shape, 1)
    step = 1
    while step < v.shape[1]:
        v = v + jnp.where(lane >= step, pltpu.roll(v, step, 1), 0.0)
        step *= 2
    return v


def rates(side, log_decay, across):
    def kernel(z_ref, d_ref, a_ref, all_ref, mine_ref, total_ref):
        here, there = running_sum(d_ref[...]), running_sum(a_ref[...])
        for h in range(8):
            all_ref[h] = here[h : h + 1]
        for half in range(2):

            @pl.when(z_ref[0] == half)
            def _():
                for h in range(4):
                    mine_ref[h] = here[half * 4 + h : half * 4 + h + 1]
                    mine_ref[4 + h] = there[half * 4 + h : half * 4 + h + 1]

        last = jnp.broadcast_to(here[:, TOK - 1 :], (8, 128))
        for d in range(32):
            total_ref[d] = last[d // 4 : d // 4 + 1]

    return pl.pallas_call(
        kernel,
        grid=(1,),
        in_specs=[SMEM, whole((8, TOK)), whole((8, TOK))],
        out_specs=[whole((8, 1, TOK)), whole((8, 1, TOK)), whole((32, 1, 128))],
        out_shape=[
            jax.ShapeDtypeStruct((8, 1, TOK), F32),
            jax.ShapeDtypeStruct((8, 1, TOK), F32),
            jax.ShapeDtypeStruct((32, 1, 128), F32),
        ],
        name="rates",
    )(side, log_decay, across)


def heads_of(kind):
    return [pl.BlockSpec((128, 2 * TOK), lambda i, h=h: (h * 3 + kind, 0)) for h in range(4)]


def whole(shape):
    return pl.BlockSpec(shape, lambda i: (0,) * len(shape))


def states(held, cumulated):
    def kernel(*refs):
        k_refs, v_refs, q_refs, c_ref, o_ref, q_out = refs[:4], refs[4:8], refs[8:12], *refs[12:]
        for h in range(4):
            q_out[h] = q_refs[h][...]
        dims = (((1,), (1,)), ((), ()))
        for block in range(2):
            lanes = slice(block * TOK, (block + 1) * TOK)
            for h in range(4):
                cum = c_ref[block * 4 + h]
                tail = jnp.exp(cum[:, TOK - 1 :] - cum)
                k = k_refs[h][:, lanes].astype(F32) * tail
                high = k.astype(BF16)
                low = (k - high.astype(F32)).astype(BF16)
                v = v_refs[h][:, lanes]
                update = lax.dot_general(high, v, dims, preferred_element_type=F32)
                update += lax.dot_general(low, v, dims, preferred_element_type=F32)
                o_ref[h * 4 : h * 4 + 4, block] = update.astype(BF16).reshape(4, 32, 128)

    return pl.pallas_call(
        kernel,
        grid=(1,),
        in_specs=heads_of(1)
        + heads_of(2)
        + [pl.BlockSpec((128, TOK), lambda i, h=h: (h * 3, 1)) for h in range(4)]
        + [whole((8, 1, TOK))],
        out_specs=[whole((16, 2, 32, 128)), whole((4, 128, TOK))],
        out_shape=[
            jax.ShapeDtypeStruct((16, 2, 32, 128), BF16),
            jax.ShapeDtypeStruct((4, 128, TOK), BF16),
        ],
        name="states",
    )(*[held] * 12, cumulated)


def intra(held, cumulated, block, dtype):
    def kernel(*refs):
        q_refs, k_refs, v_refs, c_ref, o_ref = refs[:4], refs[4:8], refs[8:12], refs[12], refs[13]
        for h in range(4):
            cum = c_ref[h]
            cum_col = jnp.transpose(jnp.broadcast_to(cum, (128, TOK)))
            for j in range(4):
                lanes = slice(j * 128, (j + 1) * 128)
                count = (j + 1) * 128
                scores = lax.dot_general(
                    k_refs[h][:, :count],
                    q_refs[h][:, lanes],
                    (((0,), (0,)), ((), ())),
                    preferred_element_type=F32,
                )
                spread = cum[:, lanes] - cum_col[:count]
                s = lax.broadcasted_iota(jnp.int32, (count, 128), 0)
                t = lax.broadcasted_iota(jnp.int32, (count, 128), 1) + j * 128
                decay = jnp.exp(jnp.where(s <= t, spread, -1e30))
                weights = (scores * decay).astype(BF16)
                inside = jnp.dot(v_refs[h][:, :count], weights, preferred_element_type=F32)
                o_ref[h, :, lanes] = inside.astype(dtype)

    return pl.pallas_call(
        kernel,
        grid=(1,),
        in_specs=[
            pl.BlockSpec((128, TOK), lambda i, h=h, kind=kind: (h * 3 + kind, block))
            for kind in range(3)
            for h in range(4)
        ]
        + [pl.BlockSpec((4, 1, TOK), lambda i: (block, 0, 0))],
        out_specs=whole((4, 128, TOK)),
        out_shape=jax.ShapeDtypeStruct((4, 128, TOK), dtype),
        name="intra",
    )(*[held] * 12, cumulated)


def carries(order, totals, pieces):
    def kernel(n_ref, d_ref, s_ref, o_ref):
        state = jnp.zeros((32, 128), F32)
        for b in range(32):
            z, yc = b // 8, b % 8
            o_ref[b] = state.astype(BF16)
            piece = s_ref[n_ref[2 * z] * 8 + yc, n_ref[2 * z + 1]]
            state = jnp.exp(d_ref[b]) * state + piece.astype(F32)

    return pl.pallas_call(
        kernel,
        grid=(1,),
        in_specs=[SMEM, whole((32, 1, 128)), whole((16, 2, 32, 128))],
        out_specs=whole((32, 32, 128)),
        out_shape=jax.ShapeDtypeStruct((32, 32, 128), BF16),
        name="carries",
    )(order, totals, pieces)


def finish(half, queries, cumulated, inside, carried, gains, output):
    def kernel(z_ref, *refs):
        q_refs, (c_ref, i_ref, s_ref, g_ref), o_ref = refs[: len(queries)], refs[len(queries) :][:4], refs[-1]
        for h in range(4):
            q = q_refs[h][...] if len(queries) == 4 else q_refs[0][h]
            carry = s_ref[4 * h : 4 * h + 4].reshape(128, 128)
            outer = lax.dot_general(carry, q, (((0,), (0,)), ((), ())), preferred_element_type=F32)
            combined = i_ref[h].astype(F32) + outer * jnp.exp(c_ref[h])
            root = lax.rsqrt(jnp.mean(combined * combined, axis=0, keepdims=True) + 1e-05)
            gain = g_ref[pl.ds(z_ref[0] * 4 + h, 1), :]
            o_ref[:, h * 128 : (h + 1) * 128] = (jnp.transpose(combined * root) * gain).astype(BF16)

    if len(queries) == 4:
        q_specs = [pl.BlockSpec((128, TOK), lambda i, z, h=h: (h * 3, 0)) for h in range(4)]
    else:
        q_specs = [pl.BlockSpec((4, 128, TOK), lambda i, z: (0, 0, 0))]
    in_specs = q_specs + [
        pl.BlockSpec((4, 1, TOK), lambda i, z: (z[0], 0, 0)),
        pl.BlockSpec((4, 128, TOK), lambda i, z: (0, 0, 0)),
        pl.BlockSpec((16, 32, 128), lambda i, z: (z[0], 0, 0)),
        pl.BlockSpec((8, 128), lambda i, z: (0, 0)),
    ]
    args = [half, *queries, cumulated, inside, carried, gains]
    aliases = {}
    if output is not None:
        in_specs.append(pl.BlockSpec(memory_space=pl.ANY))
        aliases = {len(args): 0}
        args.append(output)
    return pl.pallas_call(
        kernel,
        grid_spec=pltpu.PrefetchScalarGridSpec(
            num_scalar_prefetch=1,
            grid=(1,),
            in_specs=in_specs,
            out_specs=pl.BlockSpec((TOK, 512), lambda i, z: (0, z[0])),
        ),
        out_shape=jax.ShapeDtypeStruct((TOK, 1024), BF16),
        input_output_aliases=aliases,
        name="finish",
    )(*args)


def shards(inputs, qkv_weight, log_decay, out_gain):
    x = lax.axis_index("x")
    zh = lax.axis_index("zh")
    zl = lax.axis_index("zl")
    y = lax.axis_index("y")
    c = lax.axis_index("c")
    side = 1 - 2 * c

    order = jnp.where(zh == 0, jnp.array([0, 0, 1, 0, 1, 1, 0, 1]), jnp.array([1, 1, 0, 1, 0, 0, 1, 0]))
    order = order.astype(jnp.int32)
    mine, other = zh.astype(jnp.int32).reshape(1), (1 - zh).astype(jnp.int32).reshape(1)

    def unit(row, shift, core):
        return (row * 4 + (y + shift) % 4) * 2 + core

    zi, cs = 1 - zl, 1 - c
    rows = [
        unit(zl, 0, c),
        unit(zl, 0, cs),
        unit(zl, -side, c),
        unit(zl, side, cs),
        unit(zl, side, c),
        unit(zl, -side, cs),
        unit(zi, 0, c),
        unit(zi, 0, cs),
        unit(zl, 2, c),
        unit(zl, 2, cs),
        unit(zi, -side, c),
        unit(zi, side, cs),
        unit(zi, side, c),
        unit(zi, -side, cs),
        unit(zi, 2, c),
        unit(zi, 2, cs),
    ]
    quarters = [q % 4 for q in (x, x - side, x + side, x + 2)]
    scalars = jnp.stack(rows + quarters).astype(jnp.int32)

    own = qkv_weight.T
    quarter = lax.dynamic_slice(inputs, (128 * x, 0), (128, DIM))
    cut = SPLIT * KB
    w_a = y_move(own, 1)
    w_b = y_move(own, -1)
    w_z = z_in(own)
    log_decay_across = z_out(log_decay)
    a0 = z_out(quarter[:, :cut])
    a1 = z_out(quarter[:, cut:])
    s_own = core_swap(own)
    xa0 = x_move(a0, 1)
    xb0 = x_move(a0, -1)
    cumulated_here, cumulated, totals = rates(mine, log_decay, log_decay_across)
    totals = exchange(totals, SEQ)
    w_a, totals, scalars, order = lax.optimization_barrier((w_a, totals, scalars, order))
    w_c = y_move(w_a, 1)
    w_zb = y_move(w_z, -1)
    w_za = z_in(w_a)
    s_a = core_swap(w_a)
    s_b = core_swap(w_b)
    s_z = core_swap(w_z)
    xc0 = x_move(xa0, 1)
    xa1 = x_move(a1, 1)
    xb1 = x_move(a1, -1)
    w_zbb = y_move(w_zb, -1)
    s_c = core_swap(w_c)
    s_zb = core_swap(w_zb)
    s_za = core_swap(w_za)
    xc1 = x_move(xa1, 1)
    s_zbb = core_swap(w_zbb)

    weights = [own, s_own, w_a, s_a, w_b, s_b, w_z, s_z, w_c, s_c, w_za, s_za, w_zb, s_zb, w_zbb, s_zbb]
    units = [(w, i) for i, w in enumerate(weights)]
    here, across = [inputs], [a0, xa0, xb0, xc0, a1, xa1, xb1, xc1]
    held = project(scalars, [here], units[:8], [(0, range(8))], None)
    held = project(scalars, [here], units[8:14], [(0, range(6))], held)
    held = project(scalars, [here, across], units, [(1, range(16)), (0, (14, 15))], held)

    own_states, queries = states(held, cumulated)
    update = exchange(own_states, GROUP)
    over_queries = z_out(queries)
    inside_across = intra(held, cumulated, 1, BF16)
    over_inside = z_out(inside_across)
    running = carries(order, totals, update)
    carried = exchange(running, SEQ)
    inside = intra(held, cumulated, 0, F32)
    carried, inside = lax.optimization_barrier((carried, inside))
    output = finish(mine, [held] * 4, cumulated_here, inside, carried, out_gain, None)
    over_queries, over_inside, output = lax.optimization_barrier((over_queries, over_inside, output))
    return finish(other, [over_queries], cumulated_here, over_inside, carried, out_gain, output)


def solution(mesh):
    fine = Mesh(mesh.devices.reshape(4, 2, 2, 4, 2), ("x", "zh", "zl", "y", "c"))
    seq = ("zh", "zl", "y", "c")
    in_specs = (P(seq, None), P(None, ("x",) + seq), P("x", seq), P("x", None))
    return jax.shard_map(shards, mesh=fine, in_specs=in_specs, out_specs=P(seq, "x"), check_vma=False)
```

```python
import jax
import jax.numpy as jnp
from jax import lax
from jax.experimental import pallas as pl
from jax.experimental.pallas import tpu as pltpu
from jax.sharding import Mesh
from jax.sharding import PartitionSpec as P


F32 = jnp.float32
BF16 = jnp.bfloat16
TOK = 512
DIM = 6144
UNIT = 96
KB = 1536
NK = DIM // KB
CUTS = (0, 1, 2, 4)
GROUP = ("zl", "y", "c")
SEQ = ("zh", "zl", "y", "c")


def ring_pairs(step):
    return [
        (i * 2 + c, ((i + (step if c == 0 else -step)) % 4) * 2 + c) for i in range(4) for c in range(2)
    ]


def y_move(v, step):
    return lax.ppermute(v, ("y", "c"), ring_pairs(step))


def x_move(v, step):
    return lax.ppermute(v, ("x", "c"), ring_pairs(step))


def z_in(v):
    return lax.ppermute(v, "zl", [(0, 1), (1, 0)])


def z_out(v):
    return lax.ppermute(v, ("zh", "zl"), [(i, 3 - i) for i in range(4)])


def exchange(v, axes):
    return lax.all_to_all(v, axes, 0, 0, tiled=True)


def core_swap(v):
    return lax.ppermute(v, "c", [(0, 1), (1, 0)])


def project(scalars, blocks, units, jobs, held):
    flat = [a for arrays in blocks for a in arrays]
    count = sum(len(u) for _, u in jobs)
    both = len(blocks) == 2

    def kernel(s_ref, *refs):
        x_refs, refs = refs[: len(flat)], refs[len(flat) :]
        w_refs, refs = refs[: len(units)], refs[len(units) :]
        if held is not None:
            refs = refs[1:]
        u_ref, refs = refs[0], refs[1:]
        if both:
            across_ref, query_ref, refs = refs[0], refs[1], refs[2:]
        sem, accs, stage, refs = refs[0], refs[1 : 1 + len(jobs)], refs[1 + len(jobs)], refs[2 + len(jobs) :]
        k = pl.program_id(0)
        values = [x_refs[0]]
        if both:
            buf = refs[0]
            for n in range(len(CUTS) - 1):

                @pl.when((k >= CUTS[n]) & (k < CUTS[n + 1]))
                def _():
                    for p in range(4):
                        row = pl.multiple_of(s_ref[16 + p] * 128, 128)
                        buf[pl.ds(row, 128), :] = x_refs[1 + 4 * n + p][...]

            values.append(buf)
        for (block, members), acc in zip(jobs, accs):
            w = jnp.concatenate([w_refs[m][...] for m in members], axis=0)
            part = lax.dot_general(
                w, values[block][...], (((1,), (1,)), ((), ())), preferred_element_type=F32
            )

            @pl.when(k == 0)
            def _():
                acc[...] = part

            @pl.when(k > 0)
            def _():
                acc[...] += part

        @pl.when(k == NK - 1)
        def _():
            copies = []
            for (block, members), acc in zip(jobs, accs):
                for i, m in enumerate(members):
                    rows = slice(i * UNIT, (i + 1) * UNIT)
                    v = acc[rows, :]
                    v = (v * jax.nn.sigmoid(v)).astype(BF16)
                    at = pl.ds(pl.multiple_of(s_ref[units[m][1]] * UNIT, UNIT), UNIT)
                    if block == 1:
                        across_ref[at, :] = v
                        continue
                    stage[rows, :] = v
                    copy = pltpu.make_async_copy(stage.at[rows, :], u_ref.at[at, :], sem.at[i])
                    copy.start()
                    copies.append(copy)
            if both:
                for h in range(4):
                    query_ref[h] = across_ref[h * 384 : h * 384 + 128, :]
            for copy in copies:
                copy.wait()

    in_specs = [pl.BlockSpec((TOK, KB), lambda k, s: (0, k))]
    if both:
        for n in range(len(CUTS) - 1):
            low, last = CUTS[n], CUTS[n + 1] - CUTS[n] - 1
            in_specs += [
                pl.BlockSpec((128, KB), lambda k, s, low=low, last=last: (0, jnp.clip(k - low, 0, last)))
            ] * 4
    in_specs += [pl.BlockSpec((UNIT, KB), lambda k, s: (0, k))] * len(units)
    own_count = sum(len(u) for block, u in jobs if block == 0)
    scratch = [pltpu.SemaphoreType.DMA((own_count,))]
    scratch += [pltpu.VMEM((len(u) * UNIT, TOK), F32) for _, u in jobs]
    scratch += [pltpu.VMEM((own_count * UNIT, TOK), BF16)]
    out_specs = [pl.BlockSpec(memory_space=pl.ANY)]
    out_shape = [jax.ShapeDtypeStruct((16 * UNIT, TOK), BF16)]
    if both:
        scratch.append(pltpu.VMEM((TOK, KB), BF16))
        out_specs.append(pl.BlockSpec((16 * UNIT, TOK), lambda k, s: (0, 0)))
        out_specs.append(pl.BlockSpec((4, 128, TOK), lambda k, s: (0, 0, 0)))
        out_shape.append(jax.ShapeDtypeStruct((16 * UNIT, TOK), BF16))
        out_shape.append(jax.ShapeDtypeStruct((4, 128, TOK), BF16))
    args = [scalars, *flat, *[w for w, _ in units]]
    aliases = {}
    if held is not None:
        in_specs.append(pl.BlockSpec(memory_space=pl.ANY))
        aliases = {len(args): 0}
        args.append(held)
    return pl.pallas_call(
        kernel,
        grid_spec=pltpu.PrefetchScalarGridSpec(
            num_scalar_prefetch=1,
            grid=(NK,),
            in_specs=in_specs,
            out_specs=out_specs,
            scratch_shapes=scratch,
        ),
        out_shape=out_shape,
        input_output_aliases=aliases,
        cost_estimate=pl.CostEstimate(
            flops=2 * count * UNIT * TOK * DIM,
            bytes_accessed=2 * DIM * (len(units) * UNIT + TOK * len(blocks)),
            transcendentals=count * UNIT * TOK,
        ),
        name="project",
    )(*args)


SMEM = pl.BlockSpec(memory_space=pltpu.SMEM)


def running_sum(v):
    lane = lax.broadcasted_iota(jnp.int32, v.shape, 1)
    step = 1
    while step < v.shape[1]:
        v = v + jnp.where(lane >= step, pltpu.roll(v, step, 1), 0.0)
        step *= 2
    return v


def whole(shape):
    return pl.BlockSpec(shape, lambda i: (0,) * len(shape))


def heads_of(kind):
    return [pl.BlockSpec((128, TOK), lambda i, h=h: (h * 3 + kind, 0)) for h in range(4)]


def rates(log_decay):
    def kernel(d_ref, all_ref, total_ref):
        here = running_sum(d_ref[...])
        for h in range(8):
            all_ref[h] = here[h : h + 1]
        last = jnp.broadcast_to(here[:, TOK - 1 :], (8, 128))
        for d in range(32):
            total_ref[d] = last[d // 4 : d // 4 + 1]

    return pl.pallas_call(
        kernel,
        grid=(1,),
        in_specs=[whole((8, TOK))],
        out_specs=[whole((8, 1, TOK)), whole((32, 1, 128))],
        out_shape=[jax.ShapeDtypeStruct((8, 1, TOK), F32), jax.ShapeDtypeStruct((32, 1, 128), F32)],
        name="rates",
    )(log_decay)


def states(half, pairs):
    def kernel(z_ref, *refs):
        o_ref = refs[-1]
        dims = (((1,), (1,)), ((), ()))
        for block in range(2):
            k_refs, v_refs, c_ref = refs[9 * block :][:4], refs[9 * block + 4 :][:4], refs[9 * block + 8]
            for h in range(4):
                cum = c_ref[z_ref[0] * 4 + h]
                tail = jnp.exp(cum[:, TOK - 1 :] - cum)
                k = k_refs[h][...].astype(F32) * tail
                high = k.astype(BF16)
                low = (k - high.astype(F32)).astype(BF16)
                v = v_refs[h][...]
                update = lax.dot_general(high, v, dims, preferred_element_type=F32)
                update += lax.dot_general(low, v, dims, preferred_element_type=F32)
                o_ref[h * 4 : h * 4 + 4, block] = update.astype(BF16).reshape(4, 32, 128)

    return pl.pallas_call(
        kernel,
        grid=(1,),
        in_specs=[SMEM] + (heads_of(1) + heads_of(2) + [whole((8, 1, TOK))]) * 2,
        out_specs=whole((16, 2, 32, 128)),
        out_shape=jax.ShapeDtypeStruct((16, 2, 32, 128), BF16),
        name="states",
    )(half, *[a for projected, sums in pairs for a in [projected] * 8 + [sums]])


def intra(half, projected, sums, dtype):
    def kernel(z_ref, *refs):
        q_refs, k_refs, v_refs, c_ref, o_ref = refs[:4], refs[4:8], refs[8:12], refs[12], refs[13]
        for h in range(4):
            cum = c_ref[z_ref[0] * 4 + h]
            cum_col = jnp.transpose(jnp.broadcast_to(cum, (128, TOK)))
            for j in range(4):
                lanes = slice(j * 128, (j + 1) * 128)
                count = (j + 1) * 128
                scores = lax.dot_general(
                    k_refs[h][:, :count],
                    q_refs[h][:, lanes],
                    (((0,), (0,)), ((), ())),
                    preferred_element_type=F32,
                )
                spread = cum[:, lanes] - cum_col[:count]
                s = lax.broadcasted_iota(jnp.int32, (count, 128), 0)
                t = lax.broadcasted_iota(jnp.int32, (count, 128), 1) + j * 128
                decay = jnp.exp(jnp.where(s <= t, spread, -1e30))
                weights = (scores * decay).astype(BF16)
                inside = jnp.dot(v_refs[h][:, :count], weights, preferred_element_type=F32)
                o_ref[h, :, lanes] = inside.astype(dtype)

    return pl.pallas_call(
        kernel,
        grid=(1,),
        in_specs=[SMEM] + heads_of(0) + heads_of(1) + heads_of(2) + [whole((8, 1, TOK))],
        out_specs=whole((4, 128, TOK)),
        out_shape=jax.ShapeDtypeStruct((4, 128, TOK), dtype),
        name="intra",
    )(half, *[projected] * 12, sums)


def carries(order, totals, pieces):
    def kernel(n_ref, d_ref, s_ref, o_ref):
        state = jnp.zeros((32, 128), F32)
        for b in range(32):
            z, yc = b // 8, b % 8
            o_ref[b] = state.astype(BF16)
            piece = s_ref[n_ref[2 * z] * 8 + yc, n_ref[2 * z + 1]]
            state = jnp.exp(d_ref[b]) * state + piece.astype(F32)

    return pl.pallas_call(
        kernel,
        grid=(1,),
        in_specs=[SMEM, whole((32, 1, 128)), whole((16, 2, 32, 128))],
        out_specs=whole((32, 32, 128)),
        out_shape=jax.ShapeDtypeStruct((32, 32, 128), BF16),
        name="carries",
    )(order, totals, pieces)


def finish(half, queries, cumulated, inside, carried, gains, output):
    def kernel(z_ref, *refs):
        q_refs, (c_ref, i_ref, s_ref, g_ref), o_ref = refs[: len(queries)], refs[len(queries) :][:4], refs[-1]
        for h in range(4):
            q = q_refs[h][...] if len(queries) == 4 else q_refs[0][h]
            carry = s_ref[4 * h : 4 * h + 4].reshape(128, 128)
            outer = lax.dot_general(carry, q, (((0,), (0,)), ((), ())), preferred_element_type=F32)
            combined = i_ref[h].astype(F32) + outer * jnp.exp(c_ref[h])
            root = lax.rsqrt(jnp.mean(combined * combined, axis=0, keepdims=True) + 1e-05)
            gain = g_ref[pl.ds(z_ref[0] * 4 + h, 1), :]
            o_ref[:, h * 128 : (h + 1) * 128] = (jnp.transpose(combined * root) * gain).astype(BF16)

    if len(queries) == 4:
        q_specs = [pl.BlockSpec((128, TOK), lambda i, z, h=h: (h * 3, 0)) for h in range(4)]
    else:
        q_specs = [pl.BlockSpec((4, 128, TOK), lambda i, z: (0, 0, 0))]
    in_specs = q_specs + [
        pl.BlockSpec((4, 1, TOK), lambda i, z: (z[0], 0, 0)),
        pl.BlockSpec((4, 128, TOK), lambda i, z: (0, 0, 0)),
        pl.BlockSpec((16, 32, 128), lambda i, z: (z[0], 0, 0)),
        pl.BlockSpec((8, 128), lambda i, z: (0, 0)),
    ]
    args = [half, *queries, cumulated, inside, carried, gains]
    aliases = {}
    if output is not None:
        in_specs.append(pl.BlockSpec(memory_space=pl.ANY))
        aliases = {len(args): 0}
        args.append(output)
    return pl.pallas_call(
        kernel,
        grid_spec=pltpu.PrefetchScalarGridSpec(
            num_scalar_prefetch=1,
            grid=(1,),
            in_specs=in_specs,
            out_specs=pl.BlockSpec((TOK, 512), lambda i, z: (0, z[0])),
        ),
        out_shape=jax.ShapeDtypeStruct((TOK, 1024), BF16),
        input_output_aliases=aliases,
        name="finish",
    )(*args)


def shards(inputs, qkv_weight, log_decay, out_gain):
    x = lax.axis_index("x")
    zh = lax.axis_index("zh")
    zl = lax.axis_index("zl")
    y = lax.axis_index("y")
    c = lax.axis_index("c")
    side = 1 - 2 * c

    order = jnp.where(zh == 0, jnp.array([0, 0, 1, 0, 1, 1, 0, 1]), jnp.array([1, 1, 0, 1, 0, 0, 1, 0]))
    order = order.astype(jnp.int32)
    mine, other = zh.astype(jnp.int32).reshape(1), (1 - zh).astype(jnp.int32).reshape(1)

    def unit(row, shift, core):
        return (row * 4 + (y + shift) % 4) * 2 + core

    zi, cs = 1 - zl, 1 - c
    rows = [
        unit(zl, 0, c),
        unit(zl, 0, cs),
        unit(zl, -side, c),
        unit(zl, side, cs),
        unit(zl, side, c),
        unit(zl, -side, cs),
        unit(zi, 0, c),
        unit(zi, 0, cs),
        unit(zl, 2, c),
        unit(zl, 2, cs),
        unit(zi, -side, c),
        unit(zi, side, cs),
        unit(zi, side, c),
        unit(zi, -side, cs),
        unit(zi, 2, c),
        unit(zi, 2, cs),
    ]
    quarters = [q % 4 for q in (x, x - side, x + side, x + 2)]
    scalars = jnp.stack(rows + quarters).astype(jnp.int32)

    own = qkv_weight.T
    cuts = [
        lax.dynamic_slice(inputs, (128 * x, low * KB), (128, (high - low) * KB))
        for low, high in zip(CUTS, CUTS[1:])
    ]
    w_a = y_move(own, 1)
    w_b = y_move(own, -1)
    w_z = z_in(own)
    a = [z_out(cut) for cut in cuts]
    sums, totals = rates(log_decay)
    totals = exchange(totals, SEQ)
    sums_across = z_out(sums)
    s_own = core_swap(own)
    xa = [x_move(v, 1) for v in a]
    xb = [x_move(v, -1) for v in a]
    xc = [x_move(v, 1) for v in xa]
    w_a, totals, scalars, order = lax.optimization_barrier((w_a, totals, scalars, order))
    w_c = y_move(w_a, 1)
    w_zb = y_move(w_z, -1)
    w_za = z_in(w_a)
    s_a = core_swap(w_a)
    s_b = core_swap(w_b)
    s_z = core_swap(w_z)
    w_zbb = y_move(w_zb, -1)
    s_c = core_swap(w_c)
    s_zb = core_swap(w_zb)
    s_za = core_swap(w_za)
    s_zbb = core_swap(w_zbb)

    weights = [own, s_own, w_a, s_a, w_b, s_b, w_z, s_z, w_c, s_c, w_za, s_za, w_zb, s_zb, w_zbb, s_zbb]
    units = [(w, i) for i, w in enumerate(weights)]
    here, across = [inputs], [v for parts in zip(a, xa, xb, xc) for v in parts]
    (held,) = project(scalars, [here], units[:8], [(0, range(8))], None)
    (held,) = project(scalars, [here], units[8:14], [(0, range(6))], held)
    jobs = [(1, range(16)), (0, (14, 15))]
    held, held_across, queries = project(scalars, [here, across], units, jobs, held)

    over_queries = z_out(queries)
    own_states = states(mine, [(held, sums), (held_across, sums_across)])
    update = exchange(own_states, GROUP)
    inside_across = intra(mine, held_across, sums_across, BF16)
    over_inside = z_out(inside_across)
    running = carries(order, totals, update)
    carried = exchange(running, SEQ)
    inside = intra(mine, held, sums, F32)
    carried, inside = lax.optimization_barrier((carried, inside))
    output = finish(mine, [held] * 4, sums, inside, carried, out_gain, None)
    over_queries, over_inside, output = lax.optimization_barrier((over_queries, over_inside, output))
    return finish(other, [over_queries], sums, over_inside, carried, out_gain, output)


def solution(mesh):
    fine = Mesh(mesh.devices.reshape(4, 2, 2, 4, 2), ("x", "zh", "zl", "y", "c"))
    seq = ("zh", "zl", "y", "c")
    in_specs = (P(seq, None), P(None, ("x",) + seq), P("x", seq), P("x", None))
    return jax.shard_map(shards, mesh=fine, in_specs=in_specs, out_specs=P(seq, "x"), check_vma=False)
```

```python
import jax
import jax.numpy as jnp
from jax import lax
from jax.experimental import pallas as pl
from jax.experimental.pallas import tpu as pltpu
from jax.sharding import Mesh
from jax.sharding import PartitionSpec as P


F32 = jnp.float32
BF16 = jnp.bfloat16
TOK = 512
DIM = 6144
UNIT = 96
KB = 1536
NK = DIM // KB
CUTS = (0, 1, 2, 4)
GROUP = ("zl", "y", "c")
SEQ = ("zh", "zl", "y", "c")


def ring_pairs(step):
    return [
        (i * 2 + c, ((i + (step if c == 0 else -step)) % 4) * 2 + c) for i in range(4) for c in range(2)
    ]


def y_move(v, step):
    return lax.ppermute(v, ("y", "c"), ring_pairs(step))


def x_move(v, step):
    return lax.ppermute(v, ("x", "c"), ring_pairs(step))


def z_in(v):
    return lax.ppermute(v, "zl", [(0, 1), (1, 0)])


def z_out(v):
    return lax.ppermute(v, ("zh", "zl"), [(i, 3 - i) for i in range(4)])


def exchange(v, axes):
    return lax.all_to_all(v, axes, 0, 0, tiled=True)


def core_swap(v):
    return lax.ppermute(v, "c", [(0, 1), (1, 0)])


def grouped(members):
    parts = -(-len(members) // 7)
    size = -(-len(members) // parts)
    return [range(g, min(g + size, len(members))) for g in range(0, len(members), size)]


def project(scalars, here, cuts, units, jobs, held, partial):
    kinds = [job[0] for job in jobs]
    after = "across" in kinds

    def kernel(s_ref, x_ref, *refs):
        cut_refs, refs = refs[: 4 * len(cuts)], refs[4 * len(cuts) :]
        w_refs, refs = refs[: len(units)], refs[len(units) :]
        if partial is not None:
            partial_ref, refs = refs[0], refs[1:]
        if held is not None:
            refs = refs[1:]
        u_ref, refs = refs[0], refs[1:]
        if "start" in kinds:
            start_ref, refs = refs[0], refs[1:]
        if after:
            across_ref, query_ref, refs = refs[0], refs[1], refs[2:]
        sem, stage, accs = refs[0], refs[1], refs[2:]
        k = pl.program_id(0)

        def run(step):
            copies = []
            cut = max(n for n in range(len(CUTS) - 1) if CUTS[n] <= step)
            for (kind, members, first, last), acc in zip(jobs, accs):
                if not first <= step <= last:
                    continue
                if kind == "start":
                    acc = start_ref
                for group in grouped(members):
                    rows = slice(group[0] * UNIT, (group[-1] + 1) * UNIT)
                    w = jnp.concatenate([w_refs[members[g]][...] for g in group], axis=0)
                    if kind == "own":
                        x = x_ref[...]
                    else:
                        x = jnp.concatenate([r[...] for r in cut_refs[4 * cut : 4 * cut + 4]], axis=0)
                    v = lax.dot_general(w, x, (((1,), (1,)), ((), ())), preferred_element_type=F32)
                    if step > first:
                        v += acc[rows, :]
                    elif kind == "resume":
                        v += partial_ref[rows, :]
                    if step < last or kind == "start":
                        acc[rows, :] = v
                        continue
                    v = (v * jax.nn.sigmoid(v)).astype(BF16)
                    for n, g in enumerate(group):
                        place = s_ref[units[members[g]][1]]
                        at = pl.ds(pl.multiple_of(place * UNIT, UNIT), UNIT)
                        one = v[n * UNIT : (n + 1) * UNIT, :]
                        if kind == "own":
                            own_rows = slice(g * UNIT, (g + 1) * UNIT)
                            stage[own_rows, :] = one
                            copies.append(pltpu.make_async_copy(stage.at[own_rows, :], u_ref.at[at, :], sem.at[g]))
                            copies[-1].start()
                            continue
                        for p in range(4):
                            lane = pl.multiple_of(s_ref[16 + p] * 128, 128)
                            across_ref[at, pl.ds(lane, 128)] = one[:, p * 128 : (p + 1) * 128]
            if after and step == NK - 1:
                for h in range(4):
                    query_ref[h] = across_ref[h * 384 : h * 384 + 128, :]
            for copy in copies:
                copy.wait()

        for step in range(NK):
            pl.when(k == step)(lambda step=step: run(step))

    in_specs = [pl.BlockSpec((TOK, KB), lambda k, s: (0, k))]
    for n in range(len(cuts)):
        low, top = CUTS[n], CUTS[n + 1] - CUTS[n] - 1
        in_specs += [pl.BlockSpec((128, KB), lambda k, s, low=low, top=top: (0, jnp.clip(k - low, 0, top)))] * 4
    for m in range(len(units)):
        low = min(first for _, members, first, _ in jobs if m in members)
        top = max(last for _, members, _, last in jobs if m in members)
        in_specs.append(pl.BlockSpec((UNIT, KB), lambda k, s, low=low, top=top: (0, jnp.clip(k, low, top))))
    own_count = sum(len(members) for kind, members, _, _ in jobs if kind == "own")
    scratch = [pltpu.SemaphoreType.DMA((own_count,)), pltpu.VMEM((own_count * UNIT, TOK), BF16)]
    out_specs = [pl.BlockSpec(memory_space=pl.ANY)]
    out_shape = [jax.ShapeDtypeStruct((16 * UNIT, TOK), BF16)]
    for kind, members, _, _ in jobs:
        rows = len(members) * UNIT
        scratch.append(pltpu.VMEM((rows if kind != "start" else 8, TOK), F32))
        if kind == "start":
            out_specs.append(pl.BlockSpec((rows, TOK), lambda k, s: (0, 0)))
            out_shape.append(jax.ShapeDtypeStruct((rows, TOK), F32))
    if after:
        out_specs.append(pl.BlockSpec((16 * UNIT, TOK), lambda k, s: (0, 0)))
        out_specs.append(pl.BlockSpec((4, 128, TOK), lambda k, s: (0, 0, 0)))
        out_shape.append(jax.ShapeDtypeStruct((16 * UNIT, TOK), BF16))
        out_shape.append(jax.ShapeDtypeStruct((4, 128, TOK), BF16))
    args = [scalars, here, *[v for quarters in cuts for v in quarters], *[w for w, _ in units]]
    if partial is not None:
        in_specs.append(pl.BlockSpec(partial.shape, lambda k, s: (0, 0)))
        args.append(partial)
    aliases = {}
    if held is not None:
        in_specs.append(pl.BlockSpec(memory_space=pl.ANY))
        aliases = {len(args): 0}
        args.append(held)
    products = sum(len(members) * (last + 1 - first) for _, members, first, last in jobs) * UNIT * TOK
    return pl.pallas_call(
        kernel,
        grid_spec=pltpu.PrefetchScalarGridSpec(
            num_scalar_prefetch=1,
            grid=(NK,),
            in_specs=in_specs,
            out_specs=out_specs,
            scratch_shapes=scratch,
        ),
        out_shape=out_shape,
        input_output_aliases=aliases,
        cost_estimate=pl.CostEstimate(
            flops=2 * products * KB,
            bytes_accessed=2 * DIM * len(units) * UNIT,
            transcendentals=products // NK,
        ),
        name="project",
    )(*args)


SMEM = pl.BlockSpec(memory_space=pltpu.SMEM)


def running_sum(v):
    lane = lax.broadcasted_iota(jnp.int32, v.shape, 1)
    step = 1
    while step < v.shape[1]:
        v = v + jnp.where(lane >= step, pltpu.roll(v, step, 1), 0.0)
        step *= 2
    return v


def whole(shape):
    return pl.BlockSpec(shape, lambda i: (0,) * len(shape))


def heads_of(kind):
    return [pl.BlockSpec((128, TOK), lambda i, h=h: (h * 3 + kind, 0)) for h in range(4)]


def rates(log_decay):
    def kernel(d_ref, all_ref, total_ref):
        here = running_sum(d_ref[...])
        for h in range(8):
            all_ref[h] = here[h : h + 1]
        last = jnp.broadcast_to(here[:, TOK - 1 :], (8, 128))
        for d in range(32):
            total_ref[d] = last[d // 4 : d // 4 + 1]

    return pl.pallas_call(
        kernel,
        grid=(1,),
        in_specs=[whole((8, TOK))],
        out_specs=[whole((8, 1, TOK)), whole((32, 1, 128))],
        out_shape=[jax.ShapeDtypeStruct((8, 1, TOK), F32), jax.ShapeDtypeStruct((32, 1, 128), F32)],
        name="rates",
    )(log_decay)


def states(half, pairs):
    def kernel(z_ref, *refs):
        o_ref = refs[-1]
        dims = (((1,), (1,)), ((), ()))
        for block in range(2):
            k_refs, v_refs, c_ref = refs[9 * block :][:4], refs[9 * block + 4 :][:4], refs[9 * block + 8]
            for h in range(4):
                cum = c_ref[z_ref[0] * 4 + h]
                tail = jnp.exp(cum[:, TOK - 1 :] - cum)
                k = k_refs[h][...].astype(F32) * tail
                high = k.astype(BF16)
                low = (k - high.astype(F32)).astype(BF16)
                v = v_refs[h][...]
                update = lax.dot_general(high, v, dims, preferred_element_type=F32)
                update += lax.dot_general(low, v, dims, preferred_element_type=F32)
                o_ref[h * 4 : h * 4 + 4, block] = update.astype(BF16).reshape(4, 32, 128)

    return pl.pallas_call(
        kernel,
        grid=(1,),
        in_specs=[SMEM] + (heads_of(1) + heads_of(2) + [whole((8, 1, TOK))]) * 2,
        out_specs=whole((16, 2, 32, 128)),
        out_shape=jax.ShapeDtypeStruct((16, 2, 32, 128), BF16),
        name="states",
    )(half, *[a for projected, sums in pairs for a in [projected] * 8 + [sums]])


def intra(half, projected, sums, dtype):
    def kernel(z_ref, *refs):
        q_refs, k_refs, v_refs, c_ref, o_ref = refs[:4], refs[4:8], refs[8:12], refs[12], refs[13]
        for h in range(4):
            cum = c_ref[z_ref[0] * 4 + h]
            cum_col = jnp.transpose(jnp.broadcast_to(cum, (128, TOK)))
            for j in range(4):
                lanes = slice(j * 128, (j + 1) * 128)
                count = (j + 1) * 128
                scores = lax.dot_general(
                    k_refs[h][:, :count],
                    q_refs[h][:, lanes],
                    (((0,), (0,)), ((), ())),
                    preferred_element_type=F32,
                )
                spread = cum[:, lanes] - cum_col[:count]
                s = lax.broadcasted_iota(jnp.int32, (count, 128), 0)
                t = lax.broadcasted_iota(jnp.int32, (count, 128), 1) + j * 128
                decay = jnp.exp(jnp.where(s <= t, spread, -1e30))
                weights = (scores * decay).astype(BF16)
                inside = jnp.dot(v_refs[h][:, :count], weights, preferred_element_type=F32)
                o_ref[h, :, lanes] = inside.astype(dtype)

    return pl.pallas_call(
        kernel,
        grid=(1,),
        in_specs=[SMEM] + heads_of(0) + heads_of(1) + heads_of(2) + [whole((8, 1, TOK))],
        out_specs=whole((4, 128, TOK)),
        out_shape=jax.ShapeDtypeStruct((4, 128, TOK), dtype),
        name="intra",
    )(half, *[projected] * 12, sums)


def carries(order, totals, pieces):
    def kernel(n_ref, d_ref, s_ref, o_ref):
        state = jnp.zeros((32, 128), F32)
        for b in range(32):
            z, yc = b // 8, b % 8
            o_ref[b] = state.astype(BF16)
            piece = s_ref[n_ref[2 * z] * 8 + yc, n_ref[2 * z + 1]]
            state = jnp.exp(d_ref[b]) * state + piece.astype(F32)

    return pl.pallas_call(
        kernel,
        grid=(1,),
        in_specs=[SMEM, whole((32, 1, 128)), whole((16, 2, 32, 128))],
        out_specs=whole((32, 32, 128)),
        out_shape=jax.ShapeDtypeStruct((32, 32, 128), BF16),
        name="carries",
    )(order, totals, pieces)


def finish(half, held, over_queries, sums, inside, over_inside, carried, gains):
    def kernel(z_ref, *refs):
        q_refs, (over_ref, c_ref, in_ref, over_in_ref, s_ref, g_ref, o_ref) = refs[:4], refs[4:]
        for side in range(2):
            for h in range(4):
                head = (z_ref[0] if side == 0 else 1 - z_ref[0]) * 4 + h
                q = q_refs[h][...] if side == 0 else over_ref[h]
                within = in_ref[h] if side == 0 else over_in_ref[h].astype(F32)
                carry = s_ref[pl.ds(4 * head, 4)].reshape(128, 128)
                outer = lax.dot_general(carry, q, (((0,), (0,)), ((), ())), preferred_element_type=F32)
                combined = within + outer * jnp.exp(c_ref[head])
                root = lax.rsqrt(jnp.mean(combined * combined, axis=0, keepdims=True) + 1e-05)
                result = jnp.transpose(combined * root) * g_ref[pl.ds(head, 1), :]
                o_ref[:, pl.ds(pl.multiple_of(head * 128, 128), 128)] = result.astype(BF16)

    return pl.pallas_call(
        kernel,
        grid=(1,),
        in_specs=[SMEM]
        + heads_of(0)
        + [whole(a.shape) for a in (over_queries, sums, inside, over_inside, carried, gains)],
        out_specs=whole((TOK, 1024)),
        out_shape=jax.ShapeDtypeStruct((TOK, 1024), BF16),
        name="finish",
    )(half, *[held] * 4, over_queries, sums, inside, over_inside, carried, gains)


def shards(inputs, qkv_weight, log_decay, out_gain):
    x = lax.axis_index("x")
    zh = lax.axis_index("zh")
    zl = lax.axis_index("zl")
    y = lax.axis_index("y")
    c = lax.axis_index("c")
    side = 1 - 2 * c

    order = jnp.where(zh == 0, jnp.array([0, 0, 1, 0, 1, 1, 0, 1]), jnp.array([1, 1, 0, 1, 0, 0, 1, 0]))
    order = order.astype(jnp.int32)
    mine, other = zh.astype(jnp.int32).reshape(1), (1 - zh).astype(jnp.int32).reshape(1)

    def unit(row, shift, core):
        return (row * 4 + (y + shift) % 4) * 2 + core

    zi, cs = 1 - zl, 1 - c
    rows = [
        unit(zl, 0, c),
        unit(zl, 0, cs),
        unit(zl, -side, c),
        unit(zl, side, cs),
        unit(zl, side, c),
        unit(zl, -side, cs),
        unit(zi, 0, c),
        unit(zi, 0, cs),
        unit(zl, 2, c),
        unit(zl, 2, cs),
        unit(zi, -side, c),
        unit(zi, side, cs),
        unit(zi, side, c),
        unit(zi, -side, cs),
        unit(zi, 2, c),
        unit(zi, 2, cs),
    ]
    quarters = [q % 4 for q in (x, x - side, x + side, x + 2)]
    scalars = jnp.stack(rows + quarters).astype(jnp.int32)

    own = qkv_weight.T
    cuts = [
        lax.dynamic_slice(inputs, (128 * x, low * KB), (128, (high - low) * KB))
        for low, high in zip(CUTS, CUTS[1:])
    ]
    w_a = y_move(own, 1)
    w_b = y_move(own, -1)
    w_z = z_in(own)
    a = [z_out(cut) for cut in cuts]
    sums, totals = rates(log_decay)
    totals = exchange(totals, SEQ)
    sums_across = z_out(sums)
    s_own = core_swap(own)
    xa = [x_move(v, 1) for v in a]
    xb = [x_move(v, -1) for v in a]
    xc = [x_move(v, 1) for v in xa]
    w_a, scalars, order = lax.optimization_barrier((w_a, scalars, order))
    w_c = y_move(w_a, 1)
    w_zb = y_move(w_z, -1)
    w_za = z_in(w_a)
    s_a = core_swap(w_a)
    s_b = core_swap(w_b)
    s_z = core_swap(w_z)
    w_zbb = y_move(w_zb, -1)
    s_c = core_swap(w_c)
    s_zb = core_swap(w_zb)
    s_za = core_swap(w_za)
    s_zbb = core_swap(w_zbb)

    weights = [own, s_own, w_a, s_a, w_b, s_b, w_z, s_z, w_c, s_c, w_za, s_za, w_zb, s_zb, w_zbb, s_zbb]
    units = [(w, i) for i, w in enumerate(weights)]
    cuts = list(zip(a, xa, xb, xc))
    late = NK // 2
    jobs = [("own", range(8), 0, NK - 1)]
    (held,) = project(scalars, inputs, [], units[:8], jobs, None, None)
    jobs = [("own", range(8, 14), 0, NK - 1), ("start", range(14), 0, late - 1)]
    held, partial = project(scalars, inputs, cuts[:-1], units[:14], jobs, held, None)
    jobs = [("across", (14, 15), 0, NK - 1), ("own", (14, 15), 0, NK - 1), ("resume", range(14), late, NK - 1)]
    held, held_across, queries = project(scalars, inputs, cuts, units, jobs, held, partial)

    over_queries = z_out(queries)
    own_states = states(mine, [(held, sums), (held_across, sums_across)])
    update = exchange(own_states, GROUP)
    inside_across = intra(mine, held_across, sums_across, BF16)
    over_inside = z_out(inside_across)
    running = carries(order, totals, update)
    carried = exchange(running, SEQ)
    inside = intra(mine, held, sums, F32)
    return finish(mine, held, over_queries, sums, inside, over_inside, carried, out_gain)


def solution(mesh):
    fine = Mesh(mesh.devices.reshape(4, 2, 2, 4, 2), ("x", "zh", "zl", "y", "c"))
    seq = ("zh", "zl", "y", "c")
    in_specs = (P(seq, None), P(None, ("x",) + seq), P("x", seq), P("x", None))
    return jax.shard_map(shards, mesh=fine, in_specs=in_specs, out_specs=P(seq, "x"), check_vma=False)
```

```python
import jax
import jax.numpy as jnp
from jax import lax
from jax.experimental import pallas as pl
from jax.experimental.pallas import tpu as pltpu
from jax.sharding import Mesh
from jax.sharding import PartitionSpec as P


F32 = jnp.float32
BF16 = jnp.bfloat16
TOK = 512
DIM = 6144
UNIT = 96
KB = 1536
NK = DIM // KB
CUTS = (0, 1, 2, 4)
GROUP = ("zl", "y", "c")
SEQ = ("zh", "zl", "y", "c")


def ring_pairs(step):
    return [
        (i * 2 + c, ((i + (step if c == 0 else -step)) % 4) * 2 + c) for i in range(4) for c in range(2)
    ]


def y_move(v, step):
    return lax.ppermute(v, ("y", "c"), ring_pairs(step))


def x_move(v, step):
    return lax.ppermute(v, ("x", "c"), ring_pairs(step))


def z_in(v):
    return lax.ppermute(v, "zl", [(0, 1), (1, 0)])


def z_out(v):
    return lax.ppermute(v, ("zh", "zl"), [(i, 3 - i) for i in range(4)])


def exchange(v, axes):
    return lax.all_to_all(v, axes, 0, 0, tiled=True)


def core_swap(v):
    return lax.ppermute(v, "c", [(0, 1), (1, 0)])


def grouped(members):
    parts = -(-len(members) // 7)
    size = -(-len(members) // parts)
    return [range(g, min(g + size, len(members))) for g in range(0, len(members), size)]


def project(scalars, here, cuts, units, jobs, held, partials):
    kinds = [job[0] for job in jobs]
    after = "across" in kinds

    def kernel(s_ref, x_ref, *refs):
        cut_refs, refs = refs[: 4 * len(cuts)], refs[4 * len(cuts) :]
        w_refs, refs = refs[: len(units)], refs[len(units) :]
        partial_refs, refs = list(refs[: len(partials)]), refs[len(partials) :]
        if held is not None:
            refs = refs[1:]
        u_ref, refs = refs[0], refs[1:]
        if "start" in kinds:
            start_ref, refs = refs[0], refs[1:]
        if after:
            across_ref, query_ref, refs = refs[0], refs[1], refs[2:]
        sem, stage, accs = refs[0], refs[1], refs[2:]
        k = pl.program_id(0)
        sums_of = [partial_refs.pop(0) if kind == "resume" else None for kind in kinds]

        def run(step):
            copies = []
            cut = max(n for n in range(len(CUTS) - 1) if CUTS[n] <= step)
            for (kind, members, first, last), acc, before in zip(jobs, accs, sums_of):
                if not first <= step <= last:
                    continue
                if kind == "start":
                    acc = start_ref
                for group in grouped(members):
                    rows = slice(group[0] * UNIT, (group[-1] + 1) * UNIT)
                    w = jnp.concatenate([w_refs[members[g]][...] for g in group], axis=0)
                    if kind == "own":
                        x = x_ref[...]
                    else:
                        x = jnp.concatenate([r[...] for r in cut_refs[4 * cut : 4 * cut + 4]], axis=0)
                    v = lax.dot_general(w, x, (((1,), (1,)), ((), ())), preferred_element_type=F32)
                    if step > first:
                        v += acc[rows, :]
                    elif kind == "resume":
                        v += before[rows, :]
                    if step < last or kind == "start":
                        acc[rows, :] = v
                        continue
                    v = (v * jax.nn.sigmoid(v)).astype(BF16)
                    for n, g in enumerate(group):
                        place = s_ref[units[members[g]][1]]
                        at = pl.ds(pl.multiple_of(place * UNIT, UNIT), UNIT)
                        one = v[n * UNIT : (n + 1) * UNIT, :]
                        if kind == "own":
                            own_rows = slice(g * UNIT, (g + 1) * UNIT)
                            stage[own_rows, :] = one
                            copies.append(pltpu.make_async_copy(stage.at[own_rows, :], u_ref.at[at, :], sem.at[g]))
                            copies[-1].start()
                            continue
                        for p in range(4):
                            lane = pl.multiple_of(s_ref[16 + p] * 128, 128)
                            across_ref[at, pl.ds(lane, 128)] = one[:, p * 128 : (p + 1) * 128]
            if after and step == NK - 1:
                for h in range(4):
                    query_ref[h] = across_ref[h * 384 : h * 384 + 128, :]
            for copy in copies:
                copy.wait()

        for step in range(NK):
            pl.when(k == step)(lambda step=step: run(step))

    in_specs = [pl.BlockSpec((TOK, KB), lambda k, s: (0, k))]
    for n in range(len(cuts)):
        low, top = CUTS[n], CUTS[n + 1] - CUTS[n] - 1
        in_specs += [pl.BlockSpec((128, KB), lambda k, s, low=low, top=top: (0, jnp.clip(k - low, 0, top)))] * 4
    for m in range(len(units)):
        low = min(first for _, members, first, _ in jobs if m in members)
        top = max(last for _, members, _, last in jobs if m in members)
        in_specs.append(pl.BlockSpec((UNIT, KB), lambda k, s, low=low, top=top: (0, jnp.clip(k, low, top))))
    own_count = sum(len(members) for kind, members, _, _ in jobs if kind == "own")
    scratch = [pltpu.SemaphoreType.DMA((own_count,)), pltpu.VMEM((own_count * UNIT, TOK), BF16)]
    out_specs = [pl.BlockSpec(memory_space=pl.ANY)]
    out_shape = [jax.ShapeDtypeStruct((16 * UNIT, TOK), BF16)]
    for kind, members, _, _ in jobs:
        rows = len(members) * UNIT
        scratch.append(pltpu.VMEM((rows if kind != "start" else 8, TOK), F32))
        if kind == "start":
            out_specs.append(pl.BlockSpec((rows, TOK), lambda k, s: (0, 0)))
            out_shape.append(jax.ShapeDtypeStruct((rows, TOK), F32))
    if after:
        out_specs.append(pl.BlockSpec((16 * UNIT, TOK), lambda k, s: (0, 0)))
        out_specs.append(pl.BlockSpec((4, 128, TOK), lambda k, s: (0, 0, 0)))
        out_shape.append(jax.ShapeDtypeStruct((16 * UNIT, TOK), BF16))
        out_shape.append(jax.ShapeDtypeStruct((4, 128, TOK), BF16))
    args = [scalars, here, *[v for quarters in cuts for v in quarters], *[w for w, _ in units]]
    in_specs += [pl.BlockSpec(v.shape, lambda k, s: (0, 0)) for v in partials]
    args += partials
    aliases = {}
    if held is not None:
        in_specs.append(pl.BlockSpec(memory_space=pl.ANY))
        aliases = {len(args): 0}
        args.append(held)
    products = sum(len(members) * (last + 1 - first) for _, members, first, last in jobs) * UNIT * TOK
    return pl.pallas_call(
        kernel,
        grid_spec=pltpu.PrefetchScalarGridSpec(
            num_scalar_prefetch=1,
            grid=(NK,),
            in_specs=in_specs,
            out_specs=out_specs,
            scratch_shapes=scratch,
        ),
        out_shape=out_shape,
        input_output_aliases=aliases,
        cost_estimate=pl.CostEstimate(
            flops=2 * products * KB,
            bytes_accessed=2 * DIM * len(units) * UNIT,
            transcendentals=products // NK,
        ),
        name="project",
    )(*args)


SMEM = pl.BlockSpec(memory_space=pltpu.SMEM)


def running_sum(v):
    lane = lax.broadcasted_iota(jnp.int32, v.shape, 1)
    step = 1
    while step < v.shape[1]:
        v = v + jnp.where(lane >= step, pltpu.roll(v, step, 1), 0.0)
        step *= 2
    return v


def whole(shape):
    return pl.BlockSpec(shape, lambda i: (0,) * len(shape))


def heads_of(kind):
    return [pl.BlockSpec((128, TOK), lambda i, h=h: (h * 3 + kind, 0)) for h in range(4)]


def rates(log_decay):
    def kernel(d_ref, all_ref, total_ref):
        here = running_sum(d_ref[...])
        for h in range(8):
            all_ref[h] = here[h : h + 1]
        last = jnp.broadcast_to(here[:, TOK - 1 :], (8, 128))
        for d in range(32):
            total_ref[d] = last[d // 4 : d // 4 + 1]

    return pl.pallas_call(
        kernel,
        grid=(1,),
        in_specs=[whole((8, TOK))],
        out_specs=[whole((8, 1, TOK)), whole((32, 1, 128))],
        out_shape=[jax.ShapeDtypeStruct((8, 1, TOK), F32), jax.ShapeDtypeStruct((32, 1, 128), F32)],
        name="rates",
    )(log_decay)


def states(half, pairs):
    def kernel(z_ref, *refs):
        o_ref = refs[-1]
        dims = (((1,), (1,)), ((), ()))
        for block in range(2):
            k_refs, v_refs, c_ref = refs[9 * block :][:4], refs[9 * block + 4 :][:4], refs[9 * block + 8]
            for h in range(4):
                cum = c_ref[z_ref[0] * 4 + h]
                tail = jnp.exp(cum[:, TOK - 1 :] - cum)
                k = k_refs[h][...].astype(F32) * tail
                high = k.astype(BF16)
                low = (k - high.astype(F32)).astype(BF16)
                v = v_refs[h][...]
                update = lax.dot_general(high, v, dims, preferred_element_type=F32)
                update += lax.dot_general(low, v, dims, preferred_element_type=F32)
                o_ref[h * 4 : h * 4 + 4, block] = update.astype(BF16).reshape(4, 32, 128)

    return pl.pallas_call(
        kernel,
        grid=(1,),
        in_specs=[SMEM] + (heads_of(1) + heads_of(2) + [whole((8, 1, TOK))]) * 2,
        out_specs=whole((16, 2, 32, 128)),
        out_shape=jax.ShapeDtypeStruct((16, 2, 32, 128), BF16),
        name="states",
    )(half, *[a for projected, sums in pairs for a in [projected] * 8 + [sums]])


def intra(half, projected, sums, dtype):
    def kernel(z_ref, *refs):
        q_refs, k_refs, v_refs, c_ref, o_ref = refs[:4], refs[4:8], refs[8:12], refs[12], refs[13]
        for h in range(4):
            cum = c_ref[z_ref[0] * 4 + h]
            cum_col = jnp.transpose(jnp.broadcast_to(cum, (128, TOK)))
            for j in range(4):
                lanes = slice(j * 128, (j + 1) * 128)
                count = (j + 1) * 128
                scores = lax.dot_general(
                    k_refs[h][:, :count],
                    q_refs[h][:, lanes],
                    (((0,), (0,)), ((), ())),
                    preferred_element_type=F32,
                )
                spread = cum[:, lanes] - cum_col[:count]
                s = lax.broadcasted_iota(jnp.int32, (count, 128), 0)
                t = lax.broadcasted_iota(jnp.int32, (count, 128), 1) + j * 128
                decay = jnp.exp(jnp.where(s <= t, spread, -1e30))
                weights = (scores * decay).astype(BF16)
                inside = jnp.dot(v_refs[h][:, :count], weights, preferred_element_type=F32)
                o_ref[h, :, lanes] = inside.astype(dtype)

    return pl.pallas_call(
        kernel,
        grid=(1,),
        in_specs=[SMEM] + heads_of(0) + heads_of(1) + heads_of(2) + [whole((8, 1, TOK))],
        out_specs=whole((4, 128, TOK)),
        out_shape=jax.ShapeDtypeStruct((4, 128, TOK), dtype),
        name="intra",
    )(half, *[projected] * 12, sums)


def carries(order, totals, pieces):
    def kernel(n_ref, d_ref, s_ref, o_ref):
        state = jnp.zeros((32, 128), F32)
        for b in range(32):
            z, yc = b // 8, b % 8
            o_ref[b] = state.astype(BF16)
            piece = s_ref[n_ref[2 * z] * 8 + yc, n_ref[2 * z + 1]]
            state = jnp.exp(d_ref[b]) * state + piece.astype(F32)

    return pl.pallas_call(
        kernel,
        grid=(1,),
        in_specs=[SMEM, whole((32, 1, 128)), whole((16, 2, 32, 128))],
        out_specs=whole((32, 32, 128)),
        out_shape=jax.ShapeDtypeStruct((32, 32, 128), BF16),
        name="carries",
    )(order, totals, pieces)


def finish(half, held, over_queries, sums, inside, over_inside, carried, gains):
    def kernel(z_ref, *refs):
        q_refs, (over_ref, c_ref, in_ref, over_in_ref, s_ref, g_ref, o_ref) = refs[:4], refs[4:]
        for side in range(2):
            for h in range(4):
                head = (z_ref[0] if side == 0 else 1 - z_ref[0]) * 4 + h
                q = q_refs[h][...] if side == 0 else over_ref[h]
                within = in_ref[h] if side == 0 else over_in_ref[h].astype(F32)
                carry = s_ref[pl.ds(4 * head, 4)].reshape(128, 128)
                outer = lax.dot_general(carry, q, (((0,), (0,)), ((), ())), preferred_element_type=F32)
                combined = within + outer * jnp.exp(c_ref[head])
                root = lax.rsqrt(jnp.mean(combined * combined, axis=0, keepdims=True) + 1e-05)
                result = jnp.transpose(combined * root) * g_ref[pl.ds(head, 1), :]
                o_ref[:, pl.ds(pl.multiple_of(head * 128, 128), 128)] = result.astype(BF16)

    return pl.pallas_call(
        kernel,
        grid=(1,),
        in_specs=[SMEM]
        + heads_of(0)
        + [whole(a.shape) for a in (over_queries, sums, inside, over_inside, carried, gains)],
        out_specs=whole((TOK, 1024)),
        out_shape=jax.ShapeDtypeStruct((TOK, 1024), BF16),
        name="finish",
    )(half, *[held] * 4, over_queries, sums, inside, over_inside, carried, gains)


def shards(inputs, qkv_weight, log_decay, out_gain):
    x = lax.axis_index("x")
    zh = lax.axis_index("zh")
    zl = lax.axis_index("zl")
    y = lax.axis_index("y")
    c = lax.axis_index("c")
    side = 1 - 2 * c

    order = jnp.where(zh == 0, jnp.array([0, 0, 1, 0, 1, 1, 0, 1]), jnp.array([1, 1, 0, 1, 0, 0, 1, 0]))
    order = order.astype(jnp.int32)
    mine, other = zh.astype(jnp.int32).reshape(1), (1 - zh).astype(jnp.int32).reshape(1)

    def unit(row, shift, core):
        return (row * 4 + (y + shift) % 4) * 2 + core

    zi, cs = 1 - zl, 1 - c
    rows = [
        unit(zl, 0, c),
        unit(zl, 0, cs),
        unit(zl, -side, c),
        unit(zl, side, cs),
        unit(zl, side, c),
        unit(zl, -side, cs),
        unit(zi, 0, c),
        unit(zi, 0, cs),
        unit(zl, 2, c),
        unit(zl, 2, cs),
        unit(zi, -side, c),
        unit(zi, side, cs),
        unit(zi, side, c),
        unit(zi, -side, cs),
        unit(zi, 2, c),
        unit(zi, 2, cs),
    ]
    quarters = [q % 4 for q in (x, x - side, x + side, x + 2)]
    scalars = jnp.stack(rows + quarters).astype(jnp.int32)

    own = qkv_weight.T
    cuts = [
        lax.dynamic_slice(inputs, (128 * x, low * KB), (128, (high - low) * KB))
        for low, high in zip(CUTS, CUTS[1:])
    ]
    w_a = y_move(own, 1)
    w_b = y_move(own, -1)
    w_z = z_in(own)
    a = [z_out(cut) for cut in cuts]
    sums, totals = rates(log_decay)
    totals = exchange(totals, SEQ)
    sums_across = z_out(sums)
    s_own = core_swap(own)
    xa = [x_move(v, 1) for v in a]
    xb = [x_move(v, -1) for v in a]
    xc = [x_move(v, 1) for v in xa]
    w_a, scalars, order = lax.optimization_barrier((w_a, scalars, order))
    w_c = y_move(w_a, 1)
    w_zb = y_move(w_z, -1)
    w_za = z_in(w_a)
    s_a = core_swap(w_a)
    s_b = core_swap(w_b)
    s_z = core_swap(w_z)
    w_zbb = y_move(w_zb, -1)
    s_c = core_swap(w_c)
    s_zb = core_swap(w_zb)
    s_za = core_swap(w_za)
    s_zbb = core_swap(w_zbb)

    weights = [own, s_own, w_a, s_a, w_b, s_b, w_z, s_z, w_c, s_c, w_za, s_za, w_zb, s_zb, w_zbb, s_zbb]
    units = [(w, i) for i, w in enumerate(weights)]
    cuts = list(zip(a, xa, xb, xc))
    late = NK // 2
    jobs = [("own", range(8), 0, NK - 1), ("start", range(8), 0, late - 1)]
    held, early = project(scalars, inputs, cuts[:-1], units[:8], jobs, None, [])
    jobs = [("own", range(6), 0, NK - 1), ("start", range(6), 0, late - 1)]
    held, middle = project(scalars, inputs, cuts[:-1], units[8:14], jobs, held, [])
    jobs = [("across", (14, 15), 0, NK - 1), ("own", (14, 15), 0, NK - 1)]
    jobs += [("resume", range(8), late, NK - 1), ("resume", range(8, 14), late, NK - 1)]
    args = (scalars, inputs, cuts, units, jobs, held, [early, middle])
    held, held_across, queries = project(*args)

    over_queries = z_out(queries)
    own_states = states(mine, [(held, sums), (held_across, sums_across)])
    update = exchange(own_states, GROUP)
    inside_across = intra(mine, held_across, sums_across, BF16)
    over_inside = z_out(inside_across)
    running = carries(order, totals, update)
    carried = exchange(running, SEQ)
    inside = intra(mine, held, sums, F32)
    return finish(mine, held, over_queries, sums, inside, over_inside, carried, out_gain)


def solution(mesh):
    fine = Mesh(mesh.devices.reshape(4, 2, 2, 4, 2), ("x", "zh", "zl", "y", "c"))
    seq = ("zh", "zl", "y", "c")
    in_specs = (P(seq, None), P(None, ("x",) + seq), P("x", seq), P("x", None))
    return jax.shard_map(shards, mesh=fine, in_specs=in_specs, out_specs=P(seq, "x"), check_vma=False)
```

```python
import jax
import jax.numpy as jnp
from jax import lax
from jax.experimental import pallas as pl
from jax.experimental.pallas import tpu as pltpu
from jax.sharding import Mesh
from jax.sharding import PartitionSpec as P


F32 = jnp.float32
BF16 = jnp.bfloat16
TOK = 512
DIM = 6144
UNIT = 96
KB = 1536
NK = DIM // KB
CUTS = (0, 1, 2, 4)
GROUP = ("zl", "y", "c")
SEQ = ("zh", "zl", "y", "c")


def ring_pairs(step):
    return [
        (i * 2 + c, ((i + (step if c == 0 else -step)) % 4) * 2 + c) for i in range(4) for c in range(2)
    ]


def y_move(v, step):
    return lax.ppermute(v, ("y", "c"), ring_pairs(step))


def x_move(v, step):
    return lax.ppermute(v, ("x", "c"), ring_pairs(step))


def z_in(v):
    return lax.ppermute(v, "zl", [(0, 1), (1, 0)])


def z_out(v):
    return lax.ppermute(v, ("zh", "zl"), [(i, 3 - i) for i in range(4)])


def exchange(v, axes):
    return lax.all_to_all(v, axes, 0, 0, tiled=True)


def core_swap(v):
    return lax.ppermute(v, "c", [(0, 1), (1, 0)])


def near(v):
    return pltpu.with_memory_space_constraint(v, pltpu.VMEM)


def grouped(members):
    parts = -(-len(members) // 7)
    size = -(-len(members) // parts)
    return [range(g, min(g + size, len(members))) for g in range(0, len(members), size)]


def project(scalars, here, cuts, units, jobs, held, partials):
    kinds = [job[0] for job in jobs]
    after = "across" in kinds

    def kernel(s_ref, x_ref, *refs):
        cut_refs, refs = refs[: 4 * len(cuts)], refs[4 * len(cuts) :]
        w_refs, refs = refs[: len(units)], refs[len(units) :]
        partial_refs, refs = list(refs[: len(partials)]), refs[len(partials) :]
        if held is not None:
            refs = refs[1:]
        u_ref, refs = refs[0], refs[1:]
        if "start" in kinds:
            start_ref, refs = refs[0], refs[1:]
        if "go" in kinds:
            go_ref, refs = refs[0], refs[1:]
        if after:
            across_ref, query_ref, refs = refs[0], refs[1], refs[2:]
        sem, stage, accs = refs[0], refs[1], refs[2:]
        k = pl.program_id(0)
        sums_of = [partial_refs.pop(0) if kind in ("resume", "go") else None for kind in kinds]

        def run(step):
            copies = []
            cut = max(n for n in range(len(CUTS) - 1) if CUTS[n] <= step)
            for (kind, members, first, last), acc, before in zip(jobs, accs, sums_of):
                if not first <= step <= last:
                    continue
                if kind in ("start", "go"):
                    acc = start_ref if kind == "start" else go_ref
                for group in grouped(members):
                    rows = slice(group[0] * UNIT, (group[-1] + 1) * UNIT)
                    w = jnp.concatenate([w_refs[members[g]][...] for g in group], axis=0)
                    if kind == "own":
                        x = x_ref[...]
                    else:
                        x = jnp.concatenate([r[...] for r in cut_refs[4 * cut : 4 * cut + 4]], axis=0)
                    v = lax.dot_general(w, x, (((1,), (1,)), ((), ())), preferred_element_type=F32)
                    if step > first:
                        v += acc[rows, :]
                    elif before is not None:
                        v += before[rows, :]
                    if step < last or kind in ("start", "go"):
                        acc[rows, :] = v
                        continue
                    v = (v * jax.nn.sigmoid(v)).astype(BF16)
                    for n, g in enumerate(group):
                        place = s_ref[units[members[g]][1]]
                        at = pl.ds(pl.multiple_of(place * UNIT, UNIT), UNIT)
                        one = v[n * UNIT : (n + 1) * UNIT, :]
                        if kind == "own":
                            own_rows = slice(g * UNIT, (g + 1) * UNIT)
                            stage[own_rows, :] = one
                            copies.append(pltpu.make_async_copy(stage.at[own_rows, :], u_ref.at[at, :], sem.at[g]))
                            copies[-1].start()
                            continue
                        for p in range(4):
                            lane = pl.multiple_of(s_ref[16 + p] * 128, 128)
                            across_ref[at, pl.ds(lane, 128)] = one[:, p * 128 : (p + 1) * 128]
            if after and step == NK - 1:
                for h in range(4):
                    query_ref[h] = across_ref[h * 384 : h * 384 + 128, :]
            for copy in copies:
                copy.wait()

        for step in range(NK):
            pl.when(k == step)(lambda step=step: run(step))

    in_specs = [pl.BlockSpec((TOK, KB), lambda k, s: (0, k))]
    for n in range(len(cuts)):
        low, top = CUTS[n], CUTS[n + 1] - CUTS[n] - 1
        in_specs += [pl.BlockSpec((128, KB), lambda k, s, low=low, top=top: (0, jnp.clip(k - low, 0, top)))] * 4
    for m in range(len(units)):
        low = min(first for _, members, first, _ in jobs if m in members)
        top = max(last for _, members, _, last in jobs if m in members)
        in_specs.append(pl.BlockSpec((UNIT, KB), lambda k, s, low=low, top=top: (0, jnp.clip(k, low, top))))
    own_count = sum(len(members) for kind, members, _, _ in jobs if kind == "own")
    scratch = [pltpu.SemaphoreType.DMA((own_count,)), pltpu.VMEM((own_count * UNIT, TOK), BF16)]
    out_specs = [pl.BlockSpec(memory_space=pl.ANY)]
    out_shape = [jax.ShapeDtypeStruct((16 * UNIT, TOK), BF16)]
    for kind, members, _, _ in jobs:
        rows = len(members) * UNIT
        scratch.append(pltpu.VMEM((8 if kind in ("start", "go") else rows, TOK), F32))
        if kind in ("start", "go"):
            out_specs.append(pl.BlockSpec((rows, TOK), lambda k, s: (0, 0)))
            out_shape.append(jax.ShapeDtypeStruct((rows, TOK), F32))
    if after:
        out_specs.append(pl.BlockSpec((16 * UNIT, TOK), lambda k, s: (0, 0)))
        out_specs.append(pl.BlockSpec((4, 128, TOK), lambda k, s: (0, 0, 0)))
        out_shape.append(jax.ShapeDtypeStruct((16 * UNIT, TOK), BF16))
        out_shape.append(jax.ShapeDtypeStruct((4, 128, TOK), BF16))
    args = [scalars, here, *[v for quarters in cuts for v in quarters], *[w for w, _ in units]]
    in_specs += [pl.BlockSpec(v.shape, lambda k, s: (0, 0)) for v in partials]
    args += partials
    aliases = {}
    if held is not None:
        in_specs.append(pl.BlockSpec(memory_space=pl.ANY))
        aliases = {len(args): 0}
        args.append(held)
    products = sum(len(members) * (last + 1 - first) for _, members, first, last in jobs) * UNIT * TOK
    return pl.pallas_call(
        kernel,
        grid_spec=pltpu.PrefetchScalarGridSpec(
            num_scalar_prefetch=1,
            grid=(NK,),
            in_specs=in_specs,
            out_specs=out_specs,
            scratch_shapes=scratch,
        ),
        out_shape=out_shape,
        input_output_aliases=aliases,
        cost_estimate=pl.CostEstimate(
            flops=2 * products * KB,
            bytes_accessed=2 * DIM * len(units) * UNIT,
            transcendentals=products // NK,
        ),
        name="project",
    )(*args)


SMEM = pl.BlockSpec(memory_space=pltpu.SMEM)
VMEM = pl.BlockSpec(memory_space=pltpu.VMEM)


def running_sum(v):
    lane = lax.broadcasted_iota(jnp.int32, v.shape, 1)
    step = 1
    while step < v.shape[1]:
        v = v + jnp.where(lane >= step, pltpu.roll(v, step, 1), 0.0)
        step *= 2
    return v


def whole(shape):
    return pl.BlockSpec(shape, lambda i: (0,) * len(shape))


def heads_of(kind):
    return [pl.BlockSpec((128, TOK), lambda i, h=h: (h * 3 + kind, 0)) for h in range(4)]


def rates(log_decay):
    def kernel(d_ref, all_ref, total_ref):
        here = running_sum(d_ref[...])
        for h in range(8):
            all_ref[h] = here[h : h + 1]
        last = jnp.broadcast_to(here[:, TOK - 1 :], (8, 128))
        for d in range(32):
            total_ref[d] = last[d // 4 : d // 4 + 1]

    return pl.pallas_call(
        kernel,
        grid=(1,),
        in_specs=[whole((8, TOK))],
        out_specs=[whole((8, 1, TOK)), whole((32, 1, 128))],
        out_shape=[jax.ShapeDtypeStruct((8, 1, TOK), F32), jax.ShapeDtypeStruct((32, 1, 128), F32)],
        name="rates",
    )(log_decay)


def states(half, pairs):
    def kernel(z_ref, *refs):
        o_ref = refs[-1]
        dims = (((1,), (1,)), ((), ()))
        for block in range(2):
            k_refs, v_refs, c_ref = refs[9 * block :][:4], refs[9 * block + 4 :][:4], refs[9 * block + 8]
            for h in range(4):
                cum = c_ref[z_ref[0] * 4 + h]
                tail = jnp.exp(cum[:, TOK - 1 :] - cum)
                k = k_refs[h][...].astype(F32) * tail
                high = k.astype(BF16)
                low = (k - high.astype(F32)).astype(BF16)
                v = v_refs[h][...]
                update = lax.dot_general(high, v, dims, preferred_element_type=F32)
                update += lax.dot_general(low, v, dims, preferred_element_type=F32)
                o_ref[h * 4 : h * 4 + 4, block] = update.astype(BF16).reshape(4, 32, 128)

    return pl.pallas_call(
        kernel,
        grid=(1,),
        in_specs=[SMEM] + (heads_of(1) + heads_of(2) + [whole((8, 1, TOK))]) * 2,
        out_specs=whole((16, 2, 32, 128)),
        out_shape=jax.ShapeDtypeStruct((16, 2, 32, 128), BF16),
        name="states",
    )(half, *[a for projected, sums in pairs for a in [projected] * 8 + [sums]])


def intra(half, projected, sums, dtype):
    def kernel(z_ref, *refs):
        q_refs, k_refs, v_refs, c_ref, o_ref = refs[:4], refs[4:8], refs[8:12], refs[12], refs[13]
        for h in range(4):
            cum = c_ref[z_ref[0] * 4 + h]
            cum_col = jnp.transpose(jnp.broadcast_to(cum, (128, TOK)))
            for j in range(4):
                lanes = slice(j * 128, (j + 1) * 128)
                count = (j + 1) * 128
                scores = lax.dot_general(
                    k_refs[h][:, :count],
                    q_refs[h][:, lanes],
                    (((0,), (0,)), ((), ())),
                    preferred_element_type=F32,
                )
                spread = cum[:, lanes] - cum_col[:count]
                s = lax.broadcasted_iota(jnp.int32, (count, 128), 0)
                t = lax.broadcasted_iota(jnp.int32, (count, 128), 1) + j * 128
                decay = jnp.exp(jnp.where(s <= t, spread, -1e30))
                weights = (scores * decay).astype(BF16)
                inside = jnp.dot(v_refs[h][:, :count], weights, preferred_element_type=F32)
                o_ref[h, :, lanes] = inside.astype(dtype)

    return pl.pallas_call(
        kernel,
        grid=(1,),
        in_specs=[SMEM] + heads_of(0) + heads_of(1) + heads_of(2) + [whole((8, 1, TOK))],
        out_specs=whole((4, 128, TOK)),
        out_shape=jax.ShapeDtypeStruct((4, 128, TOK), dtype),
        name="intra",
    )(half, *[projected] * 12, sums)


def carries(order, totals, pieces):
    def kernel(n_ref, d_ref, s_ref, o_ref):
        state = jnp.zeros((32, 128), F32)
        for b in range(32):
            z, yc = b // 8, b % 8
            o_ref[b] = state.astype(BF16)
            piece = s_ref[n_ref[2 * z] * 8 + yc, n_ref[2 * z + 1]]
            state = jnp.exp(d_ref[b]) * state + piece.astype(F32)

    return pl.pallas_call(
        kernel,
        grid=(1,),
        in_specs=[SMEM, VMEM, VMEM],
        out_specs=whole((32, 32, 128)),
        out_shape=jax.ShapeDtypeStruct((32, 32, 128), BF16),
        name="carries",
    )(order, near(totals), near(pieces))


def finish(half, held, over_queries, sums, inside, over_inside, carried, gains):
    def kernel(z_ref, *refs):
        q_refs, (over_ref, c_ref, in_ref, over_in_ref, s_ref, g_ref, o_ref) = refs[:4], refs[4:]
        for side in range(2):
            for h in range(4):
                head = (z_ref[0] if side == 0 else 1 - z_ref[0]) * 4 + h
                q = q_refs[h][...] if side == 0 else over_ref[h]
                within = in_ref[h] if side == 0 else over_in_ref[h].astype(F32)
                carry = s_ref[pl.ds(4 * head, 4)].reshape(128, 128)
                outer = lax.dot_general(carry, q, (((0,), (0,)), ((), ())), preferred_element_type=F32)
                combined = within + outer * jnp.exp(c_ref[head])
                root = lax.rsqrt(jnp.mean(combined * combined, axis=0, keepdims=True) + 1e-05)
                result = jnp.transpose(combined * root) * g_ref[pl.ds(head, 1), :]
                o_ref[:, pl.ds(pl.multiple_of(head * 128, 128), 128)] = result.astype(BF16)

    return pl.pallas_call(
        kernel,
        grid=(1,),
        in_specs=[SMEM]
        + heads_of(0)
        + [VMEM, whole((8, 1, TOK)), whole((4, 128, TOK)), VMEM, VMEM, whole((8, 128))],
        out_specs=whole((TOK, 1024)),
        out_shape=jax.ShapeDtypeStruct((TOK, 1024), BF16),
        name="finish",
    )(half, *[held] * 4, near(over_queries), sums, inside, near(over_inside), near(carried), gains)


def shards(inputs, qkv_weight, log_decay, out_gain):
    x = lax.axis_index("x")
    zh = lax.axis_index("zh")
    zl = lax.axis_index("zl")
    y = lax.axis_index("y")
    c = lax.axis_index("c")
    side = 1 - 2 * c

    order = jnp.where(zh == 0, jnp.array([0, 0, 1, 0, 1, 1, 0, 1]), jnp.array([1, 1, 0, 1, 0, 0, 1, 0]))
    order = order.astype(jnp.int32)
    mine, other = zh.astype(jnp.int32).reshape(1), (1 - zh).astype(jnp.int32).reshape(1)

    def unit(row, shift, core):
        return (row * 4 + (y + shift) % 4) * 2 + core

    zi, cs = 1 - zl, 1 - c
    rows = [
        unit(zl, 0, c),
        unit(zl, 0, cs),
        unit(zl, -side, c),
        unit(zl, side, cs),
        unit(zl, side, c),
        unit(zl, -side, cs),
        unit(zi, 0, c),
        unit(zi, 0, cs),
        unit(zl, 2, c),
        unit(zl, 2, cs),
        unit(zi, -side, c),
        unit(zi, side, cs),
        unit(zi, side, c),
        unit(zi, -side, cs),
        unit(zi, 2, c),
        unit(zi, 2, cs),
    ]
    quarters = [q % 4 for q in (x, x - side, x + side, x + 2)]
    scalars = jnp.stack(rows + quarters).astype(jnp.int32)

    own = qkv_weight.T
    cuts = [
        lax.dynamic_slice(inputs, (128 * x, low * KB), (128, (high - low) * KB))
        for low, high in zip(CUTS, CUTS[1:])
    ]
    w_a = y_move(own, 1)
    w_b = y_move(own, -1)
    w_z = z_in(own)
    a = [z_out(cut) for cut in cuts]
    sums, totals = rates(log_decay)
    totals = exchange(totals, SEQ)
    sums_across = z_out(sums)
    s_own = core_swap(own)
    xa = [x_move(v, 1) for v in a]
    xb = [x_move(v, -1) for v in a]
    xc = [x_move(v, 1) for v in xa]
    w_a, scalars, order = lax.optimization_barrier((w_a, scalars, order))
    w_c = y_move(w_a, 1)
    w_zb = y_move(w_z, -1)
    w_za = z_in(w_a)
    s_a = core_swap(w_a)
    s_b = core_swap(w_b)
    s_z = core_swap(w_z)
    w_zbb = y_move(w_zb, -1)
    s_c = core_swap(w_c)
    s_zb = core_swap(w_zb)
    s_za = core_swap(w_za)
    s_zbb = core_swap(w_zbb)

    weights = [own, s_own, w_a, s_a, w_b, s_b, w_z, s_z, w_c, s_c, w_za, s_za, w_zb, s_zb, w_zbb, s_zbb]
    units = [(w, i) for i, w in enumerate(weights)]
    cuts = list(zip(a, xa, xb, xc))
    late = NK // 2
    jobs = [("own", range(8), 0, NK - 1), ("start", range(8), 0, 0)]
    held, early = project(scalars, inputs, cuts[:1], units[:8], jobs, None, [])
    jobs = [("own", range(8, 14), 0, NK - 1), ("start", range(8, 14), 0, late - 1), ("go", range(8), 1, late - 1)]
    args = (scalars, inputs, cuts[:2], units[:14], jobs, held, [early])
    held, middle, early = project(*args)
    jobs = [("across", (14, 15), 0, NK - 1), ("own", (14, 15), 0, NK - 1)]
    jobs += [("resume", range(8), late, NK - 1), ("resume", range(8, 14), late, NK - 1)]
    args = (scalars, inputs, cuts, units, jobs, held, [early, middle])
    held, held_across, queries = project(*args)

    over_queries = z_out(queries)
    own_states = states(mine, [(held, sums), (held_across, sums_across)])
    update = exchange(own_states, GROUP)
    inside_across = intra(mine, held_across, sums_across, BF16)
    over_inside = z_out(inside_across)
    running = carries(order, totals, update)
    carried = exchange(running, SEQ)
    inside = intra(mine, held, sums, F32)
    return finish(mine, held, over_queries, sums, inside, over_inside, carried, out_gain)


def solution(mesh):
    fine = Mesh(mesh.devices.reshape(4, 2, 2, 4, 2), ("x", "zh", "zl", "y", "c"))
    seq = ("zh", "zl", "y", "c")
    in_specs = (P(seq, None), P(None, ("x",) + seq), P("x", seq), P("x", None))
    return jax.shard_map(shards, mesh=fine, in_specs=in_specs, out_specs=P(seq, "x"), check_vma=False)
```

```python
import jax
import jax.numpy as jnp
from jax import lax
from jax.experimental import pallas as pl
from jax.experimental.pallas import tpu as pltpu
from jax.sharding import Mesh
from jax.sharding import PartitionSpec as P


F32 = jnp.float32
BF16 = jnp.bfloat16
TOK = 512
DIM = 6144
UNIT = 96
KB = 1536
NK = DIM // KB
CUTS = (0, 1, 2, 4)
GROUP = ("zl", "y", "c")
SEQ = ("zh", "zl", "y", "c")


def ring_pairs(step):
    return [
        (i * 2 + c, ((i + (step if c == 0 else -step)) % 4) * 2 + c) for i in range(4) for c in range(2)
    ]


def y_move(v, step):
    return lax.ppermute(v, ("y", "c"), ring_pairs(step))


def x_move(v, step):
    return lax.ppermute(v, ("x", "c"), ring_pairs(step))


def z_in(v):
    return lax.ppermute(v, "zl", [(0, 1), (1, 0)])


def z_out(v):
    return lax.ppermute(v, ("zh", "zl"), [(i, 3 - i) for i in range(4)])


def exchange(v, axes):
    return lax.all_to_all(v, axes, 0, 0, tiled=True)


def core_swap(v):
    return lax.ppermute(v, "c", [(0, 1), (1, 0)])


def near(v):
    return pltpu.with_memory_space_constraint(v, pltpu.VMEM)


def grouped(members):
    parts = -(-len(members) // 7)
    size = -(-len(members) // parts)
    return [range(g, min(g + size, len(members))) for g in range(0, len(members), size)]


def project(scalars, here, cuts, units, jobs, held, partials):
    kinds = [job[0] for job in jobs]
    after = "across" in kinds

    def kernel(s_ref, x_ref, *refs):
        cut_refs, refs = refs[: 4 * len(cuts)], refs[4 * len(cuts) :]
        w_refs, refs = refs[: len(units)], refs[len(units) :]
        partial_refs, refs = list(refs[: len(partials)]), refs[len(partials) :]
        if held is not None:
            refs = refs[1:]
        u_ref, refs = refs[0], refs[1:]
        if "start" in kinds:
            start_ref, refs = refs[0], refs[1:]
        if "go" in kinds:
            go_ref, refs = refs[0], refs[1:]
        if after:
            across_ref, query_ref, refs = refs[0], refs[1], refs[2:]
        sem, stage, accs = refs[0], refs[1], refs[2:]
        k = pl.program_id(0)
        sums_of = [partial_refs.pop(0) if kind in ("resume", "go") else None for kind in kinds]

        def run(step):
            copies = []
            cut = max(n for n in range(len(CUTS) - 1) if CUTS[n] <= step)
            for (kind, members, first, last), acc, before in zip(jobs, accs, sums_of):
                if not first <= step <= last:
                    continue
                if kind in ("start", "go"):
                    acc = start_ref if kind == "start" else go_ref
                for group in grouped(members):
                    rows = slice(group[0] * UNIT, (group[-1] + 1) * UNIT)
                    w = jnp.concatenate([w_refs[members[g]][...] for g in group], axis=0)
                    if kind == "own":
                        x = x_ref[...]
                    else:
                        x = jnp.concatenate([r[...] for r in cut_refs[4 * cut : 4 * cut + 4]], axis=0)
                    v = lax.dot_general(w, x, (((1,), (1,)), ((), ())), preferred_element_type=F32)
                    if step > first:
                        v += acc[rows, :]
                    elif before is not None:
                        v += before[rows, :]
                    if step < last or kind in ("start", "go"):
                        acc[rows, :] = v
                        continue
                    v = (v * jax.nn.sigmoid(v)).astype(BF16)
                    for n, g in enumerate(group):
                        place = s_ref[units[members[g]][1]]
                        at = pl.ds(pl.multiple_of(place * UNIT, UNIT), UNIT)
                        one = v[n * UNIT : (n + 1) * UNIT, :]
                        if kind == "own":
                            own_rows = slice(g * UNIT, (g + 1) * UNIT)
                            stage[own_rows, :] = one
                            copies.append(pltpu.make_async_copy(stage.at[own_rows, :], u_ref.at[at, :], sem.at[g]))
                            copies[-1].start()
                            continue
                        for p in range(4):
                            lane = pl.multiple_of(s_ref[16 + p] * 128, 128)
                            across_ref[at, pl.ds(lane, 128)] = one[:, p * 128 : (p + 1) * 128]
            if after and step == NK - 1:
                for h in range(4):
                    query_ref[h] = across_ref[h * 384 : h * 384 + 128, :]
            for copy in copies:
                copy.wait()

        for step in range(NK):
            pl.when(k == step)(lambda step=step: run(step))

    in_specs = [pl.BlockSpec((TOK, KB), lambda k, s: (0, k))]
    for n in range(len(cuts)):
        low, top = CUTS[n], CUTS[n + 1] - CUTS[n] - 1
        in_specs += [pl.BlockSpec((128, KB), lambda k, s, low=low, top=top: (0, jnp.clip(k - low, 0, top)))] * 4
    for m in range(len(units)):
        low = min(first for _, members, first, _ in jobs if m in members)
        top = max(last for _, members, _, last in jobs if m in members)
        in_specs.append(pl.BlockSpec((UNIT, KB), lambda k, s, low=low, top=top: (0, jnp.clip(k, low, top))))
    own_count = sum(len(members) for kind, members, _, _ in jobs if kind == "own")
    scratch = [pltpu.SemaphoreType.DMA((own_count,)), pltpu.VMEM((own_count * UNIT, TOK), BF16)]
    out_specs = [pl.BlockSpec(memory_space=pl.ANY)]
    out_shape = [jax.ShapeDtypeStruct((16 * UNIT, TOK), BF16)]
    for kind, members, _, _ in jobs:
        rows = len(members) * UNIT
        scratch.append(pltpu.VMEM((8 if kind in ("start", "go") else rows, TOK), F32))
        if kind in ("start", "go"):
            out_specs.append(pl.BlockSpec(memory_space=pltpu.VMEM))
            out_shape.append(pltpu.VMEM((rows, TOK), F32))
    if after:
        out_specs.append(pl.BlockSpec((16 * UNIT, TOK), lambda k, s: (0, 0)))
        out_specs.append(pl.BlockSpec((4, 128, TOK), lambda k, s: (0, 0, 0)))
        out_shape.append(jax.ShapeDtypeStruct((16 * UNIT, TOK), BF16))
        out_shape.append(jax.ShapeDtypeStruct((4, 128, TOK), BF16))
    args = [scalars, here, *[v for quarters in cuts for v in quarters], *[w for w, _ in units]]
    in_specs += [pl.BlockSpec(memory_space=pltpu.VMEM)] * len(partials)
    args += [near(v) for v in partials]
    aliases = {}
    if held is not None:
        in_specs.append(pl.BlockSpec(memory_space=pl.ANY))
        aliases = {len(args): 0}
        args.append(held)
    products = sum(len(members) * (last + 1 - first) for _, members, first, last in jobs) * UNIT * TOK
    return pl.pallas_call(
        kernel,
        grid_spec=pltpu.PrefetchScalarGridSpec(
            num_scalar_prefetch=1,
            grid=(NK,),
            in_specs=in_specs,
            out_specs=out_specs,
            scratch_shapes=scratch,
        ),
        out_shape=out_shape,
        input_output_aliases=aliases,
        compiler_params=pltpu.CompilerParams(vmem_limit_bytes=44 * 2**20),
        cost_estimate=pl.CostEstimate(
            flops=2 * products * KB,
            bytes_accessed=2 * DIM * len(units) * UNIT,
            transcendentals=products // NK,
        ),
        name="project",
    )(*args)


SMEM = pl.BlockSpec(memory_space=pltpu.SMEM)
VMEM = pl.BlockSpec(memory_space=pltpu.VMEM)


def running_sum(v):
    lane = lax.broadcasted_iota(jnp.int32, v.shape, 1)
    step = 1
    while step < v.shape[1]:
        v = v + jnp.where(lane >= step, pltpu.roll(v, step, 1), 0.0)
        step *= 2
    return v


def whole(shape):
    return pl.BlockSpec(shape, lambda i: (0,) * len(shape))


def heads_of(kind):
    return [pl.BlockSpec((128, TOK), lambda i, h=h: (h * 3 + kind, 0)) for h in range(4)]


def rates(log_decay):
    def kernel(d_ref, all_ref, total_ref):
        here = running_sum(d_ref[...])
        for h in range(8):
            all_ref[h] = here[h : h + 1]
        last = jnp.broadcast_to(here[:, TOK - 1 :], (8, 128))
        for d in range(32):
            total_ref[d] = last[d // 4 : d // 4 + 1]

    return pl.pallas_call(
        kernel,
        grid=(1,),
        in_specs=[whole((8, TOK))],
        out_specs=[whole((8, 1, TOK)), whole((32, 1, 128))],
        out_shape=[jax.ShapeDtypeStruct((8, 1, TOK), F32), jax.ShapeDtypeStruct((32, 1, 128), F32)],
        name="rates",
    )(log_decay)


def states(half, pairs):
    def kernel(z_ref, *refs):
        o_ref = refs[-1]
        dims = (((1,), (1,)), ((), ()))
        for block in range(2):
            k_refs, v_refs, c_ref = refs[9 * block :][:4], refs[9 * block + 4 :][:4], refs[9 * block + 8]
            for h in range(4):
                cum = c_ref[z_ref[0] * 4 + h]
                tail = jnp.exp(cum[:, TOK - 1 :] - cum)
                k = k_refs[h][...].astype(F32) * tail
                high = k.astype(BF16)
                low = (k - high.astype(F32)).astype(BF16)
                v = v_refs[h][...]
                update = lax.dot_general(high, v, dims, preferred_element_type=F32)
                update += lax.dot_general(low, v, dims, preferred_element_type=F32)
                o_ref[h * 4 : h * 4 + 4, block] = update.astype(BF16).reshape(4, 32, 128)

    return pl.pallas_call(
        kernel,
        grid=(1,),
        in_specs=[SMEM] + (heads_of(1) + heads_of(2) + [whole((8, 1, TOK))]) * 2,
        out_specs=whole((16, 2, 32, 128)),
        out_shape=jax.ShapeDtypeStruct((16, 2, 32, 128), BF16),
        name="states",
    )(half, *[a for projected, sums in pairs for a in [projected] * 8 + [sums]])


def intra(half, projected, sums, dtype):
    def kernel(z_ref, *refs):
        q_refs, k_refs, v_refs, c_ref, o_ref = refs[:4], refs[4:8], refs[8:12], refs[12], refs[13]
        for h in range(4):
            cum = c_ref[z_ref[0] * 4 + h]
            cum_col = jnp.transpose(jnp.broadcast_to(cum, (128, TOK)))
            for j in range(4):
                lanes = slice(j * 128, (j + 1) * 128)
                count = (j + 1) * 128
                scores = lax.dot_general(
                    k_refs[h][:, :count],
                    q_refs[h][:, lanes],
                    (((0,), (0,)), ((), ())),
                    preferred_element_type=F32,
                )
                spread = cum[:, lanes] - cum_col[:count]
                s = lax.broadcasted_iota(jnp.int32, (count, 128), 0)
                t = lax.broadcasted_iota(jnp.int32, (count, 128), 1) + j * 128
                decay = jnp.exp(jnp.where(s <= t, spread, -1e30))
                weights = (scores * decay).astype(BF16)
                inside = jnp.dot(v_refs[h][:, :count], weights, preferred_element_type=F32)
                o_ref[h, :, lanes] = inside.astype(dtype)

    return pl.pallas_call(
        kernel,
        grid=(1,),
        in_specs=[SMEM] + heads_of(0) + heads_of(1) + heads_of(2) + [whole((8, 1, TOK))],
        out_specs=whole((4, 128, TOK)),
        out_shape=jax.ShapeDtypeStruct((4, 128, TOK), dtype),
        name="intra",
    )(half, *[projected] * 12, sums)


def carries(order, totals, pieces):
    def kernel(n_ref, d_ref, s_ref, o_ref):
        state = jnp.zeros((32, 128), F32)
        for b in range(32):
            z, yc = b // 8, b % 8
            o_ref[b] = state.astype(BF16)
            piece = s_ref[n_ref[2 * z] * 8 + yc, n_ref[2 * z + 1]]
            state = jnp.exp(d_ref[b]) * state + piece.astype(F32)

    return pl.pallas_call(
        kernel,
        grid=(1,),
        in_specs=[SMEM, VMEM, VMEM],
        out_specs=whole((32, 32, 128)),
        out_shape=jax.ShapeDtypeStruct((32, 32, 128), BF16),
        name="carries",
    )(order, near(totals), near(pieces))


def finish(half, held, over_queries, sums, inside, over_inside, carried, gains):
    def kernel(z_ref, *refs):
        q_refs, (over_ref, c_ref, in_ref, over_in_ref, s_ref, g_ref, o_ref) = refs[:4], refs[4:]
        for side in range(2):
            for h in range(4):
                head = (z_ref[0] if side == 0 else 1 - z_ref[0]) * 4 + h
                q = q_refs[h][...] if side == 0 else over_ref[h]
                within = in_ref[h] if side == 0 else over_in_ref[h].astype(F32)
                carry = s_ref[pl.ds(4 * head, 4)].reshape(128, 128)
                outer = lax.dot_general(carry, q, (((0,), (0,)), ((), ())), preferred_element_type=F32)
                combined = within + outer * jnp.exp(c_ref[head])
                root = lax.rsqrt(jnp.mean(combined * combined, axis=0, keepdims=True) + 1e-05)
                result = jnp.transpose(combined * root) * g_ref[pl.ds(head, 1), :]
                o_ref[:, pl.ds(pl.multiple_of(head * 128, 128), 128)] = result.astype(BF16)

    return pl.pallas_call(
        kernel,
        grid=(1,),
        in_specs=[SMEM]
        + heads_of(0)
        + [VMEM, whole((8, 1, TOK)), whole((4, 128, TOK)), VMEM, VMEM, whole((8, 128))],
        out_specs=whole((TOK, 1024)),
        out_shape=jax.ShapeDtypeStruct((TOK, 1024), BF16),
        name="finish",
    )(half, *[held] * 4, near(over_queries), sums, inside, near(over_inside), near(carried), gains)


def shards(inputs, qkv_weight, log_decay, out_gain):
    x = lax.axis_index("x")
    zh = lax.axis_index("zh")
    zl = lax.axis_index("zl")
    y = lax.axis_index("y")
    c = lax.axis_index("c")
    side = 1 - 2 * c

    order = jnp.where(zh == 0, jnp.array([0, 0, 1, 0, 1, 1, 0, 1]), jnp.array([1, 1, 0, 1, 0, 0, 1, 0]))
    order = order.astype(jnp.int32)
    mine, other = zh.astype(jnp.int32).reshape(1), (1 - zh).astype(jnp.int32).reshape(1)

    def unit(row, shift, core):
        return (row * 4 + (y + shift) % 4) * 2 + core

    zi, cs = 1 - zl, 1 - c
    rows = [
        unit(zl, 0, c),
        unit(zl, 0, cs),
        unit(zl, -side, c),
        unit(zl, side, cs),
        unit(zl, side, c),
        unit(zl, -side, cs),
        unit(zi, 0, c),
        unit(zi, 0, cs),
        unit(zl, 2, c),
        unit(zl, 2, cs),
        unit(zi, -side, c),
        unit(zi, side, cs),
        unit(zi, side, c),
        unit(zi, -side, cs),
        unit(zi, 2, c),
        unit(zi, 2, cs),
    ]
    quarters = [q % 4 for q in (x, x - side, x + side, x + 2)]
    scalars = jnp.stack(rows + quarters).astype(jnp.int32)

    own = qkv_weight.T
    cuts = [
        lax.dynamic_slice(inputs, (128 * x, low * KB), (128, (high - low) * KB))
        for low, high in zip(CUTS, CUTS[1:])
    ]
    w_a = y_move(own, 1)
    w_b = y_move(own, -1)
    w_z = z_in(own)
    a = [z_out(cut) for cut in cuts]
    sums, totals = rates(log_decay)
    totals = exchange(totals, SEQ)
    sums_across = z_out(sums)
    s_own = core_swap(own)
    xa = [x_move(v, 1) for v in a]
    xb = [x_move(v, -1) for v in a]
    xc = [x_move(v, 1) for v in xa]
    w_a, scalars, order = lax.optimization_barrier((w_a, scalars, order))
    w_c = y_move(w_a, 1)
    w_zb = y_move(w_z, -1)
    w_za = z_in(w_a)
    s_a = core_swap(w_a)
    s_b = core_swap(w_b)
    s_z = core_swap(w_z)
    w_zbb = y_move(w_zb, -1)
    s_c = core_swap(w_c)
    s_zb = core_swap(w_zb)
    s_za = core_swap(w_za)
    s_zbb = core_swap(w_zbb)

    weights = [own, s_own, w_a, s_a, w_b, s_b, w_z, s_z, w_c, s_c, w_za, s_za, w_zb, s_zb, w_zbb, s_zbb]
    units = [(w, i) for i, w in enumerate(weights)]
    cuts = list(zip(a, xa, xb, xc))
    late = NK // 2
    jobs = [("own", range(8), 0, NK - 1), ("start", range(8), 0, 0)]
    held, early = project(scalars, inputs, cuts[:1], units[:8], jobs, None, [])
    jobs = [("own", range(8, 14), 0, NK - 1), ("start", range(8, 14), 0, late - 1), ("go", range(8), 1, late - 1)]
    args = (scalars, inputs, cuts[:2], units[:14], jobs, held, [early])
    held, middle, early = project(*args)
    jobs = [("across", (14, 15), 0, NK - 1), ("own", (14, 15), 0, NK - 1)]
    jobs += [("resume", range(8), late, NK - 1), ("resume", range(8, 14), late, NK - 1)]
    args = (scalars, inputs, cuts, units, jobs, held, [early, middle])
    held, held_across, queries = project(*args)

    over_queries = z_out(queries)
    own_states = states(mine, [(held, sums), (held_across, sums_across)])
    update = exchange(own_states, GROUP)
    inside_across = intra(mine, held_across, sums_across, BF16)
    over_inside = z_out(inside_across)
    running = carries(order, totals, update)
    carried = exchange(running, SEQ)
    inside = intra(mine, held, sums, F32)
    return finish(mine, held, over_queries, sums, inside, over_inside, carried, out_gain)


def solution(mesh):
    fine = Mesh(mesh.devices.reshape(4, 2, 2, 4, 2), ("x", "zh", "zl", "y", "c"))
    seq = ("zh", "zl", "y", "c")
    in_specs = (P(seq, None), P(None, ("x",) + seq), P("x", seq), P("x", None))
    return jax.shard_map(shards, mesh=fine, in_specs=in_specs, out_specs=P(seq, "x"), check_vma=False)
```

```python
import jax
import jax.numpy as jnp
from jax import lax
from jax.experimental import pallas as pl
from jax.experimental.pallas import tpu as pltpu
from jax.sharding import Mesh
from jax.sharding import PartitionSpec as P


F32 = jnp.float32
BF16 = jnp.bfloat16
TOK = 512
DIM = 6144
UNIT = 96
KB = 1536
NK = DIM // KB
CUTS = (0, 1, 2, 4)
GROUP = ("zl", "y", "c")
SEQ = ("zh", "zl", "y", "c")


def ring_pairs(step):
    return [
        (i * 2 + c, ((i + (step if c == 0 else -step)) % 4) * 2 + c) for i in range(4) for c in range(2)
    ]


def y_move(v, step):
    return lax.ppermute(v, ("y", "c"), ring_pairs(step))


def x_move(v, step):
    return lax.ppermute(v, ("x", "c"), ring_pairs(step))


def z_in(v):
    return lax.ppermute(v, "zl", [(0, 1), (1, 0)])


def z_out(v):
    return lax.ppermute(v, ("zh", "zl"), [(i, 3 - i) for i in range(4)])


def exchange(v, axes):
    return lax.all_to_all(v, axes, 0, 0, tiled=True)


def core_swap(v):
    return lax.ppermute(v, "c", [(0, 1), (1, 0)])


def near(v):
    return pltpu.with_memory_space_constraint(v, pltpu.VMEM)


def grouped(members):
    parts = -(-len(members) // 7)
    size = -(-len(members) // parts)
    return [range(g, min(g + size, len(members))) for g in range(0, len(members), size)]


def project(scalars, here, cuts, units, jobs, held, partials):
    kinds = [job[0] for job in jobs]
    after = "across" in kinds

    def kernel(s_ref, x_ref, *refs):
        cut_refs, refs = refs[: 4 * len(cuts)], refs[4 * len(cuts) :]
        w_refs, refs = refs[: len(units)], refs[len(units) :]
        partial_refs, refs = list(refs[: len(partials)]), refs[len(partials) :]
        if held is not None:
            refs = refs[1:]
        u_ref, refs = refs[0], refs[1:]
        if "start" in kinds:
            start_ref, refs = refs[0], refs[1:]
        if "go" in kinds:
            go_ref, refs = refs[0], refs[1:]
        if after:
            across_ref, query_ref, refs = refs[0], refs[1], refs[2:]
        sem, stage, accs = refs[0], refs[1], refs[2:]
        k = pl.program_id(0)
        sums_of = [partial_refs.pop(0) if kind in ("resume", "go") else None for kind in kinds]

        def run(step):
            copies = []
            cut = max(n for n in range(len(CUTS) - 1) if CUTS[n] <= step)
            for (kind, members, first, last), acc, before in zip(jobs, accs, sums_of):
                if not first <= step <= last:
                    continue
                if kind in ("start", "go"):
                    acc = start_ref if kind == "start" else go_ref
                for group in grouped(members):
                    rows = slice(group[0] * UNIT, (group[-1] + 1) * UNIT)
                    w = jnp.concatenate([w_refs[members[g]][...] for g in group], axis=0)
                    if kind == "own":
                        x = x_ref[...]
                    else:
                        x = jnp.concatenate([r[...] for r in cut_refs[4 * cut : 4 * cut + 4]], axis=0)
                    v = lax.dot_general(w, x, (((1,), (1,)), ((), ())), preferred_element_type=F32)
                    if step > first:
                        v += acc[rows, :]
                    elif before is not None:
                        v += before[rows, :]
                    if step < last or kind in ("start", "go"):
                        acc[rows, :] = v
                        continue
                    v = (v * jax.nn.sigmoid(v)).astype(BF16)
                    for n, g in enumerate(group):
                        place = s_ref[units[members[g]][1]]
                        at = pl.ds(pl.multiple_of(place * UNIT, UNIT), UNIT)
                        one = v[n * UNIT : (n + 1) * UNIT, :]
                        if kind == "own":
                            own_rows = slice(g * UNIT, (g + 1) * UNIT)
                            stage[own_rows, :] = one
                            copies.append(pltpu.make_async_copy(stage.at[own_rows, :], u_ref.at[at, :], sem.at[g]))
                            copies[-1].start()
                            continue
                        for p in range(4):
                            lane = pl.multiple_of(s_ref[16 + p] * 128, 128)
                            across_ref[at, pl.ds(lane, 128)] = one[:, p * 128 : (p + 1) * 128]
            if after and step == NK - 1:
                for h in range(4):
                    query_ref[h] = across_ref[h * 384 : h * 384 + 128, :]
            for copy in copies:
                copy.wait()

        for step in range(NK):
            pl.when(k == step)(lambda step=step: run(step))

    in_specs = [pl.BlockSpec((TOK, KB), lambda k, s: (0, k))]
    for n in range(len(cuts)):
        low, top = CUTS[n], CUTS[n + 1] - CUTS[n] - 1
        in_specs += [pl.BlockSpec((128, KB), lambda k, s, low=low, top=top: (0, jnp.clip(k - low, 0, top)))] * 4
    for m in range(len(units)):
        low = min(first for _, members, first, _ in jobs if m in members)
        top = max(last for _, members, _, last in jobs if m in members)
        in_specs.append(pl.BlockSpec((UNIT, KB), lambda k, s, low=low, top=top: (0, jnp.clip(k, low, top))))
    own_count = sum(len(members) for kind, members, _, _ in jobs if kind == "own")
    scratch = [pltpu.SemaphoreType.DMA((own_count,)), pltpu.VMEM((own_count * UNIT, TOK), BF16)]
    out_specs = [pl.BlockSpec(memory_space=pl.ANY)]
    out_shape = [jax.ShapeDtypeStruct((16 * UNIT, TOK), BF16)]
    for kind, members, _, _ in jobs:
        rows = len(members) * UNIT
        scratch.append(pltpu.VMEM((8 if kind in ("start", "go") else rows, TOK), F32))
        if kind in ("start", "go"):
            out_specs.append(pl.BlockSpec(memory_space=pltpu.VMEM))
            out_shape.append(pltpu.VMEM((rows, TOK), F32))
    if after:
        out_specs.append(pl.BlockSpec((16 * UNIT, TOK), lambda k, s: (0, 0)))
        out_specs.append(pl.BlockSpec((4, 128, TOK), lambda k, s: (0, 0, 0)))
        out_shape.append(jax.ShapeDtypeStruct((16 * UNIT, TOK), BF16))
        out_shape.append(jax.ShapeDtypeStruct((4, 128, TOK), BF16))
    args = [scalars, here, *[v for quarters in cuts for v in quarters], *[w for w, _ in units]]
    in_specs += [pl.BlockSpec(memory_space=pltpu.VMEM)] * len(partials)
    args += [near(v) for v in partials]
    aliases = {}
    if held is not None:
        in_specs.append(pl.BlockSpec(memory_space=pl.ANY))
        aliases = {len(args): 0}
        args.append(held)
    need = 2 * 2 * KB * (TOK + 4 * 128 * len(cuts) + UNIT * len(units))
    need += sum(len(members) * UNIT * TOK * 4 for _, members, _, _ in jobs)
    need += (16 * UNIT + TOK) * TOK * 4 if after else 0
    products = sum(len(members) * (last + 1 - first) for _, members, first, last in jobs) * UNIT * TOK
    return pl.pallas_call(
        kernel,
        grid_spec=pltpu.PrefetchScalarGridSpec(
            num_scalar_prefetch=1,
            grid=(NK,),
            in_specs=in_specs,
            out_specs=out_specs,
            scratch_shapes=scratch,
        ),
        out_shape=out_shape,
        input_output_aliases=aliases,
        compiler_params=pltpu.CompilerParams(vmem_limit_bytes=need + 3 * 2**20),
        cost_estimate=pl.CostEstimate(
            flops=2 * products * KB,
            bytes_accessed=2 * DIM * len(units) * UNIT,
            transcendentals=products // NK,
        ),
        name="project",
    )(*args)


SMEM = pl.BlockSpec(memory_space=pltpu.SMEM)
VMEM = pl.BlockSpec(memory_space=pltpu.VMEM)


def running_sum(v):
    lane = lax.broadcasted_iota(jnp.int32, v.shape, 1)
    step = 1
    while step < v.shape[1]:
        v = v + jnp.where(lane >= step, pltpu.roll(v, step, 1), 0.0)
        step *= 2
    return v


def whole(shape):
    return pl.BlockSpec(shape, lambda i: (0,) * len(shape))


def heads_of(kind):
    return [pl.BlockSpec((128, TOK), lambda i, h=h: (h * 3 + kind, 0)) for h in range(4)]


def rates(log_decay):
    def kernel(d_ref, all_ref, total_ref):
        here = running_sum(d_ref[...])
        for h in range(8):
            all_ref[h] = here[h : h + 1]
        last = jnp.broadcast_to(here[:, TOK - 1 :], (8, 128))
        for d in range(32):
            total_ref[d] = last[d // 4 : d // 4 + 1]

    return pl.pallas_call(
        kernel,
        grid=(1,),
        in_specs=[whole((8, TOK))],
        out_specs=[whole((8, 1, TOK)), whole((32, 1, 128))],
        out_shape=[jax.ShapeDtypeStruct((8, 1, TOK), F32), jax.ShapeDtypeStruct((32, 1, 128), F32)],
        name="rates",
    )(log_decay)


def states(half, pairs):
    def kernel(z_ref, *refs):
        o_ref = refs[-1]
        dims = (((1,), (1,)), ((), ()))
        for block in range(2):
            k_refs, v_refs, c_ref = refs[9 * block :][:4], refs[9 * block + 4 :][:4], refs[9 * block + 8]
            for h in range(4):
                cum = c_ref[z_ref[0] * 4 + h]
                tail = jnp.exp(cum[:, TOK - 1 :] - cum)
                k = k_refs[h][...].astype(F32) * tail
                high = k.astype(BF16)
                low = (k - high.astype(F32)).astype(BF16)
                v = v_refs[h][...]
                update = lax.dot_general(high, v, dims, preferred_element_type=F32)
                update += lax.dot_general(low, v, dims, preferred_element_type=F32)
                o_ref[h * 4 : h * 4 + 4, block] = update.astype(BF16).reshape(4, 32, 128)

    return pl.pallas_call(
        kernel,
        grid=(1,),
        in_specs=[SMEM] + (heads_of(1) + heads_of(2) + [whole((8, 1, TOK))]) * 2,
        out_specs=whole((16, 2, 32, 128)),
        out_shape=jax.ShapeDtypeStruct((16, 2, 32, 128), BF16),
        name="states",
    )(half, *[a for projected, sums in pairs for a in [projected] * 8 + [sums]])


def intra(half, projected, sums, dtype):
    def kernel(z_ref, *refs):
        q_refs, k_refs, v_refs, c_ref, o_ref = refs[:4], refs[4:8], refs[8:12], refs[12], refs[13]
        for h in range(4):
            cum = c_ref[z_ref[0] * 4 + h]
            cum_col = jnp.transpose(jnp.broadcast_to(cum, (128, TOK)))
            for j in range(4):
                lanes = slice(j * 128, (j + 1) * 128)
                count = (j + 1) * 128
                scores = lax.dot_general(
                    k_refs[h][:, :count],
                    q_refs[h][:, lanes],
                    (((0,), (0,)), ((), ())),
                    preferred_element_type=F32,
                )
                spread = cum[:, lanes] - cum_col[:count]
                s = lax.broadcasted_iota(jnp.int32, (count, 128), 0)
                t = lax.broadcasted_iota(jnp.int32, (count, 128), 1) + j * 128
                decay = jnp.exp(jnp.where(s <= t, spread, -1e30))
                weights = (scores * decay).astype(BF16)
                inside = jnp.dot(v_refs[h][:, :count], weights, preferred_element_type=F32)
                o_ref[h, :, lanes] = inside.astype(dtype)

    return pl.pallas_call(
        kernel,
        grid=(1,),
        in_specs=[SMEM] + heads_of(0) + heads_of(1) + heads_of(2) + [whole((8, 1, TOK))],
        out_specs=whole((4, 128, TOK)),
        out_shape=jax.ShapeDtypeStruct((4, 128, TOK), dtype),
        name="intra",
    )(half, *[projected] * 12, sums)


def carries(order, totals, pieces):
    def kernel(n_ref, d_ref, s_ref, o_ref):
        state = jnp.zeros((32, 128), F32)
        for b in range(32):
            z, yc = b // 8, b % 8
            o_ref[b] = state.astype(BF16)
            piece = s_ref[n_ref[2 * z] * 8 + yc, n_ref[2 * z + 1]]
            state = jnp.exp(d_ref[b]) * state + piece.astype(F32)

    return pl.pallas_call(
        kernel,
        grid=(1,),
        in_specs=[SMEM, VMEM, VMEM],
        out_specs=whole((32, 32, 128)),
        out_shape=jax.ShapeDtypeStruct((32, 32, 128), BF16),
        name="carries",
    )(order, near(totals), near(pieces))


def finish(half, held, over_queries, sums, inside, over_inside, carried, gains):
    def kernel(z_ref, *refs):
        q_refs, (over_ref, c_ref, in_ref, over_in_ref, s_ref, g_ref, o_ref) = refs[:4], refs[4:]
        for side in range(2):
            for h in range(4):
                head = (z_ref[0] if side == 0 else 1 - z_ref[0]) * 4 + h
                q = q_refs[h][...] if side == 0 else over_ref[h]
                within = in_ref[h] if side == 0 else over_in_ref[h].astype(F32)
                carry = s_ref[pl.ds(4 * head, 4)].reshape(128, 128)
                outer = lax.dot_general(carry, q, (((0,), (0,)), ((), ())), preferred_element_type=F32)
                combined = within + outer * jnp.exp(c_ref[head])
                root = lax.rsqrt(jnp.mean(combined * combined, axis=0, keepdims=True) + 1e-05)
                result = jnp.transpose(combined * root) * g_ref[pl.ds(head, 1), :]
                o_ref[:, pl.ds(pl.multiple_of(head * 128, 128), 128)] = result.astype(BF16)

    return pl.pallas_call(
        kernel,
        grid=(1,),
        in_specs=[SMEM]
        + heads_of(0)
        + [VMEM, whole((8, 1, TOK)), whole((4, 128, TOK)), VMEM, VMEM, whole((8, 128))],
        out_specs=whole((TOK, 1024)),
        out_shape=jax.ShapeDtypeStruct((TOK, 1024), BF16),
        name="finish",
    )(half, *[held] * 4, near(over_queries), sums, inside, near(over_inside), near(carried), gains)


def shards(inputs, qkv_weight, log_decay, out_gain):
    x = lax.axis_index("x")
    zh = lax.axis_index("zh")
    zl = lax.axis_index("zl")
    y = lax.axis_index("y")
    c = lax.axis_index("c")
    side = 1 - 2 * c

    order = jnp.where(zh == 0, jnp.array([0, 0, 1, 0, 1, 1, 0, 1]), jnp.array([1, 1, 0, 1, 0, 0, 1, 0]))
    order = order.astype(jnp.int32)
    mine, other = zh.astype(jnp.int32).reshape(1), (1 - zh).astype(jnp.int32).reshape(1)

    def unit(row, shift, core):
        return (row * 4 + (y + shift) % 4) * 2 + core

    zi, cs = 1 - zl, 1 - c
    rows = [
        unit(zl, 0, c),
        unit(zl, 0, cs),
        unit(zl, -side, c),
        unit(zl, side, cs),
        unit(zl, side, c),
        unit(zl, -side, cs),
        unit(zi, 0, c),
        unit(zi, 0, cs),
        unit(zl, 2, c),
        unit(zl, 2, cs),
        unit(zi, -side, c),
        unit(zi, side, cs),
        unit(zi, side, c),
        unit(zi, -side, cs),
        unit(zi, 2, c),
        unit(zi, 2, cs),
    ]
    quarters = [q % 4 for q in (x, x - side, x + side, x + 2)]
    scalars = jnp.stack(rows + quarters).astype(jnp.int32)

    own = qkv_weight.T
    cuts = [
        lax.dynamic_slice(inputs, (128 * x, low * KB), (128, (high - low) * KB))
        for low, high in zip(CUTS, CUTS[1:])
    ]
    w_a = y_move(own, 1)
    w_b = y_move(own, -1)
    w_z = z_in(own)
    a = [z_out(cut) for cut in cuts]
    sums, totals = rates(log_decay)
    totals = exchange(totals, SEQ)
    sums_across = z_out(sums)
    s_own = core_swap(own)
    xa = [x_move(v, 1) for v in a]
    xb = [x_move(v, -1) for v in a]
    xc = [x_move(v, 1) for v in xa]
    w_a, scalars, order = lax.optimization_barrier((w_a, scalars, order))
    w_c = y_move(w_a, 1)
    w_zb = y_move(w_z, -1)
    w_za = z_in(w_a)
    s_a = core_swap(w_a)
    s_b = core_swap(w_b)
    s_z = core_swap(w_z)
    w_zbb = y_move(w_zb, -1)
    s_c = core_swap(w_c)
    s_zb = core_swap(w_zb)
    s_za = core_swap(w_za)
    s_zbb = core_swap(w_zbb)

    weights = [own, s_own, w_a, s_a, w_b, s_b, w_z, s_z, w_c, s_c, w_za, s_za, w_zb, s_zb, w_zbb, s_zbb]
    units = [(w, i) for i, w in enumerate(weights)]
    cuts = list(zip(a, xa, xb, xc))
    late = NK // 2
    jobs = [("own", range(8), 0, NK - 1), ("start", range(8), 0, 0)]
    held, early = project(scalars, inputs, cuts[:1], units[:8], jobs, None, [])
    jobs = [("own", range(8, 14), 0, NK - 1), ("start", range(8, 14), 0, late - 1), ("go", range(8), 1, late - 1)]
    args = (scalars, inputs, cuts[:2], units[:14], jobs, held, [early])
    held, middle, early = project(*args)
    jobs = [("across", (14, 15), 0, NK - 1), ("own", (14, 15), 0, NK - 1)]
    jobs += [("resume", range(8), late, NK - 1), ("resume", range(8, 14), late, NK - 1)]
    args = (scalars, inputs, cuts, units, jobs, held, [early, middle])
    held, held_across, queries = project(*args)

    over_queries = z_out(queries)
    own_states = states(mine, [(held, sums), (held_across, sums_across)])
    update = exchange(own_states, GROUP)
    inside_across = intra(mine, held_across, sums_across, BF16)
    over_inside = z_out(inside_across)
    running = carries(order, totals, update)
    carried = exchange(running, SEQ)
    inside = intra(mine, held, sums, F32)
    return finish(mine, held, over_queries, sums, inside, over_inside, carried, out_gain)


def solution(mesh):
    fine = Mesh(mesh.devices.reshape(4, 2, 2, 4, 2), ("x", "zh", "zl", "y", "c"))
    seq = ("zh", "zl", "y", "c")
    in_specs = (P(seq, None), P(None, ("x",) + seq), P("x", seq), P("x", None))
    return jax.shard_map(shards, mesh=fine, in_specs=in_specs, out_specs=P(seq, "x"), check_vma=False)
```
